32 devices in a mesh: req: 8 (over y, x, core), cand: 4 (over z).
Axes of the slice: x: 2, y: 2, z: 4, core: 2. Of those that a mesh axis runs over, the one named last changes fastest.
Arguments:
- history: bfloat16 [64, 256, 1024], P('req', 'cand'), may hold values from -6 to 6
- history_length: int32 [64], P('req'), may hold values from 32 to 256
- candidate_count: int32 [64], P('req'), may hold values from 512 to 4096
- block_shard: int32 [64, 32], P('req'), may hold values from 0 to 3, as said below
- block_index: int32 [64, 32], P('req'), may hold values from 0 to 3
- item_table: bfloat16 [16, 128, 1024], P('cand'), may hold values from -6 to 6
- item_ages: int32 [64, 4096], P('req', 'cand'), may hold values from 0 to 336
- history_weight: bfloat16 [1024, 2048], P('req'), may hold values from -0.1875 to 0.1875
- candidate_weight: bfloat16 [1024, 2048], P('req'), may hold values from -0.1875 to 0.1875
- output_weight: bfloat16 [1024, 1024], P('req'), may hold values from -0.1875 to 0.1875
- hidden_weight: bfloat16 [1024, 256], P('req'), may hold values from -0.1875 to 0.1875
- norm_gain: float32 [1024], replicated, may hold values from 0.1 to 1.9
- score_weight: bfloat16 [2, 256], replicated, may hold values from -0.375 to 0.375
Outputs:
- scores: float32 [64, 4096], P('req', 'cand')
The draws below stay inside these ranges and needn't reach their ends.
Inputs may be any that keep to these rules, and one draw needn't show every extreme that they name: `block_shard`: for each group of 8 consecutive requests (aligned) and each c, the slots j with j // 8 == c of those requests name every shard exactly 16 times.
All inputs are finite; a program needn't handle non-finite values.
Results may differ from the reference program's by a relative error of at most 0.0053.
Values may be sent and summed in bfloat16 or wider, within the bound.
A program may use at most 128 MiB of HBM per device.

```python
import math
import jax
import jax.numpy as jnp
from jax import lax

D = 1024
HEADS = 8
MLPH = 256
HIST = 256
R_DEV = 8
MAXB = 32
MINB = 4
BLOCK = 128
IB_DEV = 4
REQS = 64
SHARDS = 4
MAXC = 4096
ITEM_BLOCKS = 16
CAP = 16


def draw_history_length(key, part):
    first, second = jax.random.split(key)
    values = jax.random.randint(first, (REQS,), HIST // 8, HIST + 1)
    spot = jax.random.randint(second, (), 0, REQS)
    return jnp.where(jnp.arange(REQS) == spot, HIST, values).astype(jnp.int32)


def draw_candidate_count(key, part):
    first, second = jax.random.split(key)
    values = jax.random.randint(first, (REQS,), MINB * BLOCK, MAXC + 1)
    spot = jax.random.randint(second, (), 0, REQS)
    return jnp.where(jnp.arange(REQS) == spot, MAXC, values).astype(jnp.int32)


def draw_block_shard(key, part):
    groups = REQS // R_DEV
    per_scorer = MAXB // SHARDS
    slot_count = R_DEV * per_scorer
    ranks = jax.random.randint(key, (groups * SHARDS, slot_count), 0, 1 << 20)
    ranks = ranks * slot_count + jnp.arange(slot_count, dtype=jnp.int32)[None, :]
    order = jnp.argsort(ranks, axis=1, stable=True)
    base = jnp.arange(slot_count, dtype=jnp.int32) // CAP
    shards = base[order]
    shards = shards.reshape(groups, SHARDS, R_DEV, per_scorer).transpose(0, 2, 1, 3)
    return shards.reshape(REQS, MAXB).astype(jnp.int32)


def set_ends(entries, rng, low, top_value):
    longest = entries.shape.index(max(entries.shape))
    spots = []
    for shift in (0, 1):
        where = [jax.random.randint(jax.random.fold_in(rng, axis), (), 0, length) for axis, length in enumerate(entries.shape)]
        where[longest] = (where[longest] + shift) % entries.shape[longest]
        spots.append(tuple(where))
    return entries.at[spots[0]].set(low).at[spots[1]].set(top_value)


def shard_levels(key, shape, pieces, least, high):
    loudness = 1.0
    for dim, shards_of in pieces:
        heights = jax.random.uniform(jax.random.fold_in(jax.random.fold_in(key, 6), dim), (shards_of,), jnp.float32, least / len(pieces), high / len(pieces))
        loudness = loudness * jnp.repeat(jnp.exp(heights), shape[dim] // shards_of).reshape((-1,) + (1,) * (len(shape) - 1 - dim))
    return loudness


def noise(key, dims, width, reach, pieces=(), held_as=jnp.bfloat16):
    array = width * jax.random.normal(key, dims, jnp.float32)
    if pieces:
        array = array * shard_levels(key, dims, pieces, -0.22, 0.18)
    return jnp.clip(array, -reach, reach).astype(held_as)


def setup_inputs(seed: int = 0) -> dict:
    key_of = jax.random.split(jax.random.key(seed), 14)
    history = noise(key_of[0], (REQS, HIST, D), 1.0, 6.0, ((0, 8), (1, 4)))
    history_length = draw_history_length(jax.random.fold_in(key_of[13], 71), 0)
    candidate_count = draw_candidate_count(jax.random.fold_in(key_of[13], 71), 0)
    block_shard = draw_block_shard(jax.random.fold_in(key_of[13], 71), 0)
    block_index = set_ends(jax.random.randint(key_of[4], (REQS, MAXB), 0, IB_DEV), jax.random.fold_in(key_of[4], 1), 0, IB_DEV - 1).astype(jnp.int32)
    item_table = noise(key_of[5], (ITEM_BLOCKS, BLOCK, D), 1.0, 6.0, ((0, 4),))
    item_ages = set_ends(jax.random.randint(key_of[6], (REQS, MAXC), 0, 337), jax.random.fold_in(key_of[6], 1), 0, 336).astype(jnp.int32)
    history_weight = noise(key_of[7], (D, 2 * D), D ** -0.5, 0.1875, ((0, 8),))
    candidate_weight = noise(key_of[8], (D, 2 * D), D ** -0.5, 0.1875, ((0, 8),))
    output_weight = noise(key_of[9], (D, D), D ** -0.5, 0.1875, ((0, 8),))
    hidden_weight = noise(key_of[10], (D, MLPH), D ** -0.5, 0.1875, ((0, 8),))
    norm_gain = jnp.clip(1.0 + 0.18 * jax.random.normal(key_of[11], (D,), jnp.float32), 0.1, 1.9)
    score_weight = noise(key_of[12], (2, MLPH), MLPH ** -0.5, 0.375)
    return {"history": history, "history_length": history_length, "candidate_count": candidate_count, "block_shard": block_shard, "block_index": block_index, "item_table": item_table, "item_ages": item_ages, "history_weight": history_weight, "candidate_weight": candidate_weight, "output_weight": output_weight, "hidden_weight": hidden_weight, "norm_gain": norm_gain, "score_weight": score_weight}


EPSILON = 1e-05
AGE_SCALE = 48.0

def rounded(value):
    return lax.optimization_barrier(value.astype(jnp.bfloat16)).astype(jnp.float32)

def reference(history, history_length, candidate_count, block_shard, block_index, item_table, item_ages, history_weight, candidate_weight, output_weight, hidden_weight, norm_gain, score_weight):
    head_size = D // HEADS
    score_scale = 1.0 / math.sqrt(head_size)
    query_weight = candidate_weight[:, :D]
    gate_weight = candidate_weight[:, D:]
    positions = jnp.arange(HIST, dtype=jnp.int32)

    def one_request(operands):
        history_rows, length, row_count, sources, indices, age_rows = operands
        projected = jax.nn.silu(jnp.dot(history_rows, history_weight, preferred_element_type=jnp.float32))
        projected = rounded(projected)
        key_rows = projected[:, :D].reshape(HIST, HEADS, head_size)
        value_rows = projected[:, D:].reshape(HIST, HEADS, head_size)
        blocks = item_table[(sources * IB_DEV + indices).astype(jnp.int32)]

        def one_block(block_ops):
            block_rows, number, block_ages = block_ops

            def score_block(block_rows):
                query = rounded(jax.nn.silu(jnp.dot(block_rows, query_weight, preferred_element_type=jnp.float32)))
                query = query.reshape(BLOCK, HEADS, head_size)
                scores = jnp.einsum('ihd,phd->hip', query, key_rows) * score_scale
                weights = jax.nn.silu(scores) / length.astype(jnp.float32)
                weights = rounded(jnp.where(positions[None, None, :] < length, weights, 0.0))
                attended = jnp.einsum('hip,phd->ihd', weights, value_rows).reshape(BLOCK, D)
                gate = jax.nn.silu(jnp.dot(block_rows, gate_weight, preferred_element_type=jnp.float32))
                center = attended - lax.optimization_barrier(jnp.mean(attended, axis=-1, keepdims=True))
                spread = lax.optimization_barrier(jnp.mean(center * center, axis=-1, keepdims=True))
                normed = (center * lax.rsqrt(spread + EPSILON) * norm_gain * gate).astype(jnp.bfloat16)
                merged = (jnp.dot(normed, output_weight, preferred_element_type=jnp.float32) + block_rows.astype(jnp.float32)).astype(jnp.bfloat16)
                hidden = jax.nn.silu(jnp.dot(merged, hidden_weight, preferred_element_type=jnp.float32)).astype(jnp.bfloat16)
                logits = jnp.einsum('ik,ck->ci', hidden.astype(jnp.float32), score_weight.astype(jnp.float32))
                decays = jnp.exp(-block_ages.astype(jnp.float32) / AGE_SCALE)
                blended = decays * logits[0] + (1.0 - decays) * logits[1]
                kept_rows = number * BLOCK + jnp.arange(BLOCK, dtype=jnp.int32) < row_count
                return jnp.where(kept_rows, blended, 0.0)

            def empty_block(block_rows):
                return jnp.zeros((BLOCK,), jnp.float32)
            return lax.cond(number * BLOCK < row_count, score_block, empty_block, block_rows)
        return lax.map(one_block, (blocks, jnp.arange(MAXB, dtype=jnp.int32), age_rows.reshape(MAXB, BLOCK)))
    result = lax.map(one_request, (history, history_length, candidate_count, block_shard, block_index, item_ages))
    return result.reshape(REQS, MAXC)
```

```python
import functools
import math

import jax
import jax.numpy as jnp
from jax import lax
from jax.experimental import pallas as pl
from jax.experimental.pallas import tpu as pltpu
from jax.sharding import PartitionSpec as P

HEADS = 8
BLOCK = 128
EPSILON = 1e-05
AGE_SCALE = 48.0
PARTS = 2


def silu(value):
    half = 0.5 * value
    return half + half * jnp.tanh(half)


MESH = pl.DeviceIdType.MESH


def pair_kernel(
    groups,
    shards,
    length_ref,
    history_ref,
    item_shard_ref,
    history_shard_ref,
    candidate_shard_ref,
    output_shard_ref,
    hidden_shard_ref,
    gain_ref,
    score_weight_ref,
    logits_ref,
    events_ref,
    items_ref,
    query_weight_ref,
    key_weight_ref,
    value_weight_ref,
    gate_weight_ref,
    output_weight_ref,
    hidden_weight_ref,
    query_ref,
    gate_ref,
    pairs_ref,
    attended_ref,
    weight_send,
    weight_recv,
    pass_send,
    turn_send,
    cross_send,
    cross_recv,
    event_send,
    event_recv,
    logit_send,
    logit_recv,
    own_sem,
    own_event_sem,
):
    group = lax.axis_index("req")
    shard = lax.axis_index("cand")
    partner = group + 1 - 2 * lax.rem(group, 2)
    own_events = history_ref.shape[1]
    width = history_ref.shape[2]
    lanes = shards // PARTS
    part, lane = lax.div(shard, lanes), lax.rem(shard, lanes)
    mate = lax.rem(shard + lanes, shards)
    requests, history_total = events_ref.shape[:2]
    chunks, _, span = query_weight_ref.shape
    batches = requests // chunks
    rows = item_shard_ref.shape[0]
    head = width // HEADS
    half_scale = 0.5 / math.sqrt(head)
    depth = history_shard_ref.shape[0]
    item_depth = rows // groups
    half = groups // 2
    row, core = lax.div(group, half), lax.rem(group, 2)
    across = lax.rem(group + half, groups)
    beside = [row * half + lax.rem(group - row * half + 2 * d, half) for d in range(1, half // 2)]
    diagonal = [lax.rem(source + half, groups) for source in beside]
    near = (*beside, across)
    same_core = (*near, *diagonal)
    partner_core = [source + partner - group for source in same_core]
    others = [lax.rem(shard + d, shards) for d in range(1, shards)]
    relays = ((1, 2, 0), (2, 1, 3)) if shards == 4 else ()

    def rows_of(source):
        return pl.ds(pl.multiple_of(source * depth, depth), depth)

    def item_rows(source):
        return pl.ds(pl.multiple_of(source * item_depth, item_depth), item_depth)

    def events_of(source):
        return pl.ds(pl.multiple_of(source * own_events, own_events), own_events)

    def columns(start):
        return pl.ds(pl.multiple_of(start, span), span)

    item_piece = (
        0,
        items_ref.at[1 - part, item_rows(group)],
        lambda source: items_ref.at[1 - part, item_rows(source)],
    )

    def chunk_pieces(c):
        return (
            (
                1 + 3 * c,
                candidate_shard_ref.at[:, columns(c * span)],
                lambda source: query_weight_ref.at[c, rows_of(source)],
            ),
            (
                2 + 3 * c,
                history_shard_ref.at[:, columns(c * span)],
                lambda source: key_weight_ref.at[c, rows_of(source)],
            ),
            (
                3 + 3 * c,
                history_shard_ref.at[:, columns(width + c * span)],
                lambda source: value_weight_ref.at[c, rows_of(source)],
            ),
        )

    gate_piece = (
        1 + 3 * chunks,
        candidate_shard_ref.at[:, width:],
        lambda source: gate_weight_ref.at[rows_of(source)],
    )
    output_piece = (
        2 + 3 * chunks,
        output_shard_ref,
        lambda source: output_weight_ref.at[rows_of(source)],
    )
    hidden_piece = (
        3 + 3 * chunks,
        hidden_shard_ref,
        lambda source: hidden_weight_ref.at[rows_of(source)],
    )

    def weight_copy(piece, k, target, source):
        w, own, place = piece
        return pltpu.make_async_remote_copy(
            src_ref=own,
            dst_ref=place(source),
            send_sem=weight_send.at[w, k],
            recv_sem=weight_recv.at[w, source],
            device_id={"req": target},
            device_id_type=MESH,
        )

    def pass_copy(piece, k, source):
        w, _, place = piece
        return pltpu.make_async_remote_copy(
            src_ref=place(source),
            dst_ref=place(source),
            send_sem=pass_send.at[w, k],
            recv_sem=weight_recv.at[w, source],
            device_id={"req": partner},
            device_id_type=MESH,
        )

    def turn_copy(piece, k):
        w, _, place = piece
        source = beside[k] + core * (across - beside[k])
        target = across + core * (beside[k] - across)
        return pltpu.make_async_remote_copy(
            src_ref=place(source),
            dst_ref=place(source),
            send_sem=turn_send.at[w, k],
            recv_sem=weight_recv.at[w, source],
            device_id={"req": target},
            device_id_type=MESH,
        )

    def own_piece(piece):
        w, own, place = piece
        return pltpu.make_async_copy(own, place(group), own_sem.at[w])

    def send(pieces):
        for piece in pieces:
            for k, target in enumerate((*near, partner)):
                weight_copy(piece, k, target, group).start()

    def arrive(piece, sources):
        for source in sources:
            weight_copy(piece, 0, partner, source).wait_recv()

    def turn(pieces):
        for piece in pieces:
            arrive(piece, near)
            for k in range(len(beside)):
                turn_copy(piece, k).start()
            for k, source in enumerate(near):
                pass_copy(piece, k, source).start()

    def settle(pieces):
        for piece in pieces:
            arrive(piece, diagonal)
            for k, source in enumerate(diagonal):
                pass_copy(piece, len(near) + k, source).start()
        for piece in pieces:
            arrive(piece, (partner, *partner_core))

    def finish(pieces):
        for piece in pieces:
            for k, target in enumerate((*near, partner)):
                weight_copy(piece, k, target, group).wait_send()
            for k, source in enumerate(same_core):
                pass_copy(piece, k, source).wait_send()
            for k in range(len(beside)):
                turn_copy(piece, k).wait_send()

    def cross_copy():
        return pltpu.make_async_remote_copy(
            src_ref=item_shard_ref.at[item_rows(group)],
            dst_ref=items_ref.at[part, item_rows(group)],
            send_sem=cross_send,
            recv_sem=cross_recv,
            device_id={"cand": mate},
            device_id_type=MESH,
        )

    def cross_arrival():
        return pltpu.make_async_remote_copy(
            src_ref=item_shard_ref.at[item_rows(group)],
            dst_ref=items_ref.at[1 - part, item_rows(group)],
            send_sem=cross_send,
            recv_sem=cross_recv,
            device_id={"cand": mate},
            device_id_type=MESH,
        )

    def own_items():
        return pltpu.make_async_copy(item_shard_ref, items_ref.at[part], own_sem.at[0])

    def event_copy(i, k, target, source):
        return pltpu.make_async_remote_copy(
            src_ref=history_ref.at[lax.div(target, lanes) * requests + i],
            dst_ref=events_ref.at[i, events_of(source)],
            send_sem=event_send.at[i, k],
            recv_sem=event_recv.at[i, source],
            device_id={"cand": target},
            device_id_type=MESH,
        )

    def relay_copy(i, k):
        _, source, target = relays[k]
        return pltpu.make_async_remote_copy(
            src_ref=events_ref.at[i, events_of(source)],
            dst_ref=events_ref.at[i, events_of(source)],
            send_sem=event_send.at[i, len(others) + k],
            recv_sem=event_recv.at[i, source],
            device_id={"cand": target},
            device_id_type=MESH,
        )

    def direct(target):
        flag = shard >= 0
        for _, source, end in relays:
            flag = flag & ((shard != source) | (target != end))
        return flag

    def own_event(i):
        return pltpu.make_async_copy(
            history_ref.at[part * requests + i],
            events_ref.at[i, events_of(shard)],
            own_event_sem.at[i],
        )

    def logit_copy(i, k, target, source):
        place = logits_ref.at[lax.rem(source, lanes), lax.div(source, lanes) * requests + i]
        return pltpu.make_async_remote_copy(
            src_ref=place,
            dst_ref=place,
            send_sem=logit_send.at[i, k],
            recv_sem=logit_recv.at[i, source],
            device_id={"cand": target},
            device_id_type=MESH,
        )

    own_items().start()
    for c in range(chunks):
        for piece in chunk_pieces(c):
            own_piece(piece).start()
    for piece in (gate_piece, output_piece, hidden_piece):
        own_piece(piece).start()

    barrier = pltpu.get_barrier_semaphore()
    for target in (*near, partner):
        pl.semaphore_signal(barrier, inc=1, device_id={"req": target}, device_id_type=MESH)
    for target in others:
        pl.semaphore_signal(barrier, inc=1, device_id={"cand": target}, device_id_type=MESH)
    pl.semaphore_wait(barrier, len(near) + 1 + len(others))

    cross_copy().start()
    send(chunk_pieces(0))

    @pl.loop(0, requests)
    def _(i):
        for k, target in enumerate(others):

            @pl.when(direct(target))
            def _():
                event_copy(i, k, target, shard).start()

        own_event(i).start()

    send(chunk_pieces(1))
    cross_arrival().wait_recv()
    send((item_piece,))
    turn(chunk_pieces(0))
    if chunks > 2:
        send(chunk_pieces(2))
    turn((item_piece,))
    own_items().wait()
    settle((item_piece,))
    for c in range(chunks):
        for piece in chunk_pieces(c):
            own_piece(piece).wait()
    for piece in (gate_piece, output_piece, hidden_piece):
        own_piece(piece).wait()

    def enter_chunk(d):
        @pl.when(d + 1 < chunks)
        def _():
            turn(chunk_pieces(d + 1))

        @pl.when(d + 3 < chunks)
        def _():
            send(chunk_pieces(d + 3))

        @pl.when(d + 3 == chunks)
        def _():
            send((gate_piece,))

        @pl.when(d + 2 == chunks)
        def _():
            send((output_piece, hidden_piece))

        @pl.when(d + 1 == chunks)
        def _():
            turn((gate_piece,))

        settle(chunk_pieces(d))
        query_ref[d] = (
            half_scale
            * silu(
                jnp.dot(
                    items_ref[...].reshape(PARTS * rows, width),
                    query_weight_ref[d],
                    preferred_element_type=jnp.float32,
                )
            )
        ).astype(jnp.bfloat16)

    def enter_request(i):
        own_event(i).wait()
        for source in others:
            event_copy(i, 0, mate, source).wait_recv()
        for k, (middle, _, _) in enumerate(relays):

            @pl.when(shard == middle)
            def _():
                relay_copy(i, k).start()

    def attend(c, r, i):
        length = length_ref[part * requests + i]
        events = events_ref[i]
        pairs_ref[0] = silu(
            jnp.dot(events, key_weight_ref[c], preferred_element_type=jnp.float32)
        ).astype(jnp.bfloat16)
        live = lax.broadcasted_iota(jnp.int32, (history_total, span), 0) < length
        pairs_ref[1] = jnp.where(
            live,
            silu(jnp.dot(events, value_weight_ref[c], preferred_element_type=jnp.float32)),
            0.0,
        ).astype(jnp.bfloat16)
        for h in range(span // head):
            lanes_of = slice(h * head, (h + 1) * head)
            scores = lax.dot_general(
                query_ref[c, :, lanes_of],
                pairs_ref[0, :, lanes_of],
                (((1,), (1,)), ((), ())),
                preferred_element_type=jnp.float32,
            )
            mixed = (scores + scores * jnp.tanh(scores)).astype(jnp.bfloat16)
            attended_ref[r, c, :, lanes_of] = jnp.dot(
                mixed, pairs_ref[1, :, lanes_of], preferred_element_type=jnp.float32
            )

    def run_batch(b):
        @pl.loop(0, chunks * chunks)
        def _(t):
            d = t * 0
            for edge in range(1, chunks):
                d = d + (t >= edge * edge).astype(jnp.int32)
            k = t - d * d
            c = jnp.where(k < d, d, k - d)
            r = jnp.where(k < d, k, d)
            i = b * chunks + r

            @pl.when((k == 0) & (b == 0))
            def _():
                enter_chunk(d)

            @pl.when(k == d)
            def _():
                enter_request(i)

            attend(c, r, i)

        @pl.when(b == 0)
        def _():
            turn((output_piece, hidden_piece))
            settle((gate_piece,))
            gate_ref[...] = (
                silu(
                    jnp.dot(
                        items_ref[...].reshape(PARTS * rows, width),
                        gate_weight_ref[...],
                        preferred_element_type=jnp.float32,
                    )
                )
                * gain_ref[...]
            )
            settle((output_piece, hidden_piece))

        @pl.loop(0, chunks)
        def _(r):
            i = b * chunks + r
            length = jnp.full((1, 1), length_ref[part * requests + i], jnp.int32).astype(
                jnp.float32
            )

            @pl.loop(0, PARTS)
            def _(p):
                tile = pl.ds(pl.multiple_of(p * rows, rows), rows)
                attended = jnp.concatenate(
                    [attended_ref[r, c, tile] for c in range(chunks)], axis=-1
                )
                center = attended - jnp.mean(attended, axis=-1, keepdims=True)
                spread = jnp.mean(center * center, axis=-1, keepdims=True)
                normed = (
                    center * lax.rsqrt(spread + EPSILON * length * length) * gate_ref[tile]
                ).astype(jnp.bfloat16)
                merged = (
                    jnp.dot(normed, output_weight_ref[...], preferred_element_type=jnp.float32)
                    + items_ref[p].astype(jnp.float32)
                ).astype(jnp.bfloat16)
                hidden = silu(
                    jnp.dot(merged, hidden_weight_ref[...], preferred_element_type=jnp.float32)
                ).astype(jnp.bfloat16)
                logits_ref[lane, part * requests + i, p] = lax.dot_general(
                    score_weight_ref[...],
                    hidden,
                    (((1,), (1,)), ((), ())),
                    preferred_element_type=jnp.float32,
                )

            for k, target in enumerate(others):
                logit_copy(i, k, target, shard).start()

    if batches == 1:
        run_batch(0)
    else:

        @pl.loop(0, batches)
        def _(b):
            run_batch(b)

    cross_copy().wait_send()
    finish((item_piece, gate_piece, output_piece, hidden_piece))

    @pl.loop(0, chunks)
    def _(c):
        finish(chunk_pieces(c))

    @pl.loop(0, requests)
    def _(i):
        for k, target in enumerate(others):

            @pl.when(direct(target))
            def _():
                event_copy(i, k, target, shard).wait_send()

        for k, (middle, _, _) in enumerate(relays):

            @pl.when(shard == middle)
            def _():
                relay_copy(i, k).wait_send()

        for k, target in enumerate(others):
            logit_copy(i, k, target, shard).wait_send()
            logit_copy(i, k, target, target).wait_recv()


def pair_logits(
    history, length, items, history_weight, candidate_weight, output_weight, hidden_weight, gain,
    score_weight,
):
    all_requests, own_events, width = history.shape
    rows = items.shape[0]
    groups, shards = lax.axis_size("req"), lax.axis_size("cand")
    history_total = own_events * shards
    requests = all_requests // PARTS
    chunks = HEADS // 2
    span = width // chunks
    depth = history_weight.shape[0] * groups
    pieces = 4 + 3 * chunks
    whole = pl.BlockSpec(memory_space=pltpu.VMEM)
    apart = pl.BlockSpec(memory_space=pl.ANY)
    return pl.pallas_call(
        functools.partial(pair_kernel, groups, shards),
        out_shape=jax.ShapeDtypeStruct(
            (shards // PARTS, all_requests, PARTS, score_weight.shape[0], rows), jnp.float32
        ),
        in_specs=[
            pl.BlockSpec(memory_space=pltpu.SMEM),
            apart, apart, apart, apart, apart, apart, whole, whole,
        ],
        out_specs=whole,
        scratch_shapes=[
            pltpu.VMEM((requests, history_total, width), jnp.bfloat16),
            pltpu.VMEM((PARTS, rows, width), jnp.bfloat16),
            pltpu.VMEM((chunks, depth, span), jnp.bfloat16),
            pltpu.VMEM((chunks, depth, span), jnp.bfloat16),
            pltpu.VMEM((chunks, depth, span), jnp.bfloat16),
            pltpu.VMEM((depth, width), jnp.bfloat16),
            pltpu.VMEM((depth, width), jnp.bfloat16),
            pltpu.VMEM((depth, hidden_weight.shape[1]), jnp.bfloat16),
            pltpu.VMEM((chunks, PARTS * rows, span), jnp.bfloat16),
            pltpu.VMEM((PARTS * rows, width), jnp.float32),
            pltpu.VMEM((2, history_total, span), jnp.bfloat16),
            pltpu.VMEM((chunks, chunks, PARTS * rows, span), jnp.float32),
            pltpu.SemaphoreType.DMA((pieces, groups // 2)),
            pltpu.SemaphoreType.DMA((pieces, groups)),
            pltpu.SemaphoreType.DMA((pieces, groups // 2)),
            pltpu.SemaphoreType.DMA((pieces, groups // 2)),
            pltpu.SemaphoreType.DMA,
            pltpu.SemaphoreType.DMA,
            pltpu.SemaphoreType.DMA((requests, shards + 1)),
            pltpu.SemaphoreType.DMA((requests, shards)),
            pltpu.SemaphoreType.DMA((requests, shards)),
            pltpu.SemaphoreType.DMA((requests, shards)),
            pltpu.SemaphoreType.DMA((pieces,)),
            pltpu.SemaphoreType.DMA((requests,)),
        ],
        compiler_params=pltpu.CompilerParams(
            collective_id=0, has_side_effects=True, vmem_limit_bytes=60 * 1024 * 1024
        ),
    )(
        length, history, items, history_weight, candidate_weight, output_weight, hidden_weight,
        gain, score_weight,
    )


def blend(logits, candidate_count, block_shard, block_index, item_ages, item_blocks):
    shards = lax.axis_size("cand")
    mine = lax.axis_index("cand")
    lanes = shards // PARTS
    requests, max_blocks = block_shard.shape
    per_scorer = max_blocks // shards
    logits = logits.reshape(lanes, requests, PARTS, -1, item_blocks, BLOCK)
    ids = lax.dynamic_slice_in_dim(
        block_shard * item_blocks + block_index, mine * per_scorer, per_scorer, 1
    )
    names = (
        jnp.arange(shards * item_blocks, dtype=jnp.int32)
        .reshape(PARTS, lanes, item_blocks)
        .transpose(1, 0, 2)[:, None, :, None, :, None]
    )
    picked = ids[None, :, None, :, None, None] == names
    first, second = (
        jnp.sum(jnp.where(picked, logits[:, :, :, None, c], 0.0), axis=(0, 2, 4)) for c in (0, 1)
    )
    decays = jnp.exp(
        -item_ages.astype(jnp.float32).reshape(requests, per_scorer, BLOCK) / AGE_SCALE
    )
    blended = decays * first + (1.0 - decays) * second
    row_number = (mine * per_scorer + jnp.arange(per_scorer, dtype=jnp.int32))[
        None, :, None
    ] * BLOCK + jnp.arange(BLOCK, dtype=jnp.int32)[None, None, :]
    kept_rows = row_number < candidate_count[:, None, None]
    return jnp.where(kept_rows, blended, 0.0).reshape(requests, per_scorer * BLOCK)


def local(
    history,
    history_length,
    candidate_count,
    block_shard,
    block_index,
    item_table,
    item_ages,
    history_weight,
    candidate_weight,
    output_weight,
    hidden_weight,
    norm_gain,
    score_weight,
):
    item_blocks = item_table.shape[0]
    logits = pair_logits(
        history,
        history_length,
        item_table.reshape(-1, item_table.shape[2]),
        history_weight,
        candidate_weight,
        output_weight,
        hidden_weight,
        norm_gain[None, :],
        score_weight,
    )
    return blend(logits, candidate_count, block_shard, block_index, item_ages, item_blocks)


def solution(mesh):
    return jax.shard_map(
        local,
        mesh=mesh,
        in_specs=(
            P("req", "cand", None),
            P("req"),
            P("req"),
            P("req", None),
            P("req", None),
            P("cand", None, None),
            P("req", "cand"),
            P("req", None),
            P("req", None),
            P("req", None),
            P("req", None),
            P(),
            P(),
        ),
        out_specs=P("req", "cand"),
        check_vma=False,
    )
```

```python
import functools
import math

import jax
import jax.numpy as jnp
from jax import lax
from jax.experimental import pallas as pl
from jax.experimental.pallas import tpu as pltpu
from jax.sharding import PartitionSpec as P

HEADS = 8
BLOCK = 128
EPSILON = 1e-05
AGE_SCALE = 48.0
PARTS = 2


def silu(value):
    half = 0.5 * value
    return half + half * jnp.tanh(half)


MESH = pl.DeviceIdType.MESH


def pair_kernel(
    groups,
    shards,
    length_ref,
    history_ref,
    item_shard_ref,
    history_shard_ref,
    candidate_shard_ref,
    output_shard_ref,
    hidden_shard_ref,
    gain_ref,
    score_weight_ref,
    logits_ref,
    events_ref,
    items_ref,
    query_weight_ref,
    key_weight_ref,
    value_weight_ref,
    gate_weight_ref,
    output_weight_ref,
    hidden_weight_ref,
    query_ref,
    gate_ref,
    pairs_ref,
    attended_ref,
    normed_ref,
    weight_send,
    weight_recv,
    pass_send,
    turn_send,
    cross_send,
    cross_recv,
    event_send,
    event_recv,
    logit_send,
    logit_recv,
    own_sem,
    own_event_sem,
):
    group = lax.axis_index("req")
    shard = lax.axis_index("cand")
    partner = group + 1 - 2 * lax.rem(group, 2)
    own_events = history_ref.shape[1]
    width = history_ref.shape[2]
    lanes = shards // PARTS
    part, lane = lax.div(shard, lanes), lax.rem(shard, lanes)
    mate = lax.rem(shard + lanes, shards)
    requests, history_total = events_ref.shape[:2]
    chunks, _, span = query_weight_ref.shape
    batches = requests // chunks
    rows = item_shard_ref.shape[0]
    head = width // HEADS
    half_scale = 0.5 / math.sqrt(head)
    depth = history_shard_ref.shape[0]
    item_depth = rows // groups
    half = groups // 2
    row, core = lax.div(group, half), lax.rem(group, 2)
    across = lax.rem(group + half, groups)
    beside = [row * half + lax.rem(group - row * half + 2 * d, half) for d in range(1, half // 2)]
    diagonal = [lax.rem(source + half, groups) for source in beside]
    near = (*beside, across)
    same_core = (*near, *diagonal)
    partner_core = [source + partner - group for source in same_core]
    others = [lax.rem(shard + d, shards) for d in range(1, shards)]
    relays = ((1, 2, 0), (2, 1, 3)) if shards == 4 else ()

    def rows_of(source):
        return pl.ds(pl.multiple_of(source * depth, depth), depth)

    def item_rows(source):
        return pl.ds(pl.multiple_of(source * item_depth, item_depth), item_depth)

    def events_of(source):
        return pl.ds(pl.multiple_of(source * own_events, own_events), own_events)

    def columns(start):
        return pl.ds(pl.multiple_of(start, span), span)

    item_piece = (
        0,
        items_ref.at[1 - part, item_rows(group)],
        lambda source: items_ref.at[1 - part, item_rows(source)],
    )

    def chunk_pieces(c):
        return (
            (
                1 + 3 * c,
                candidate_shard_ref.at[:, columns(c * span)],
                lambda source: query_weight_ref.at[c, rows_of(source)],
            ),
            (
                2 + 3 * c,
                history_shard_ref.at[:, columns(c * span)],
                lambda source: key_weight_ref.at[c, rows_of(source)],
            ),
            (
                3 + 3 * c,
                history_shard_ref.at[:, columns(width + c * span)],
                lambda source: value_weight_ref.at[c, rows_of(source)],
            ),
        )

    gate_piece = (
        1 + 3 * chunks,
        candidate_shard_ref.at[:, width:],
        lambda source: gate_weight_ref.at[rows_of(source)],
    )
    output_piece = (
        2 + 3 * chunks,
        output_shard_ref,
        lambda source: output_weight_ref.at[rows_of(source)],
    )
    hidden_piece = (
        3 + 3 * chunks,
        hidden_shard_ref,
        lambda source: hidden_weight_ref.at[rows_of(source)],
    )

    def weight_copy(piece, k, target, source):
        w, own, place = piece
        return pltpu.make_async_remote_copy(
            src_ref=own,
            dst_ref=place(source),
            send_sem=weight_send.at[w, k],
            recv_sem=weight_recv.at[w, source],
            device_id={"req": target},
            device_id_type=MESH,
        )

    def pass_copy(piece, k, source):
        w, _, place = piece
        return pltpu.make_async_remote_copy(
            src_ref=place(source),
            dst_ref=place(source),
            send_sem=pass_send.at[w, k],
            recv_sem=weight_recv.at[w, source],
            device_id={"req": partner},
            device_id_type=MESH,
        )

    def turn_copy(piece, k):
        w, _, place = piece
        source = beside[k] + core * (across - beside[k])
        target = across + core * (beside[k] - across)
        return pltpu.make_async_remote_copy(
            src_ref=place(source),
            dst_ref=place(source),
            send_sem=turn_send.at[w, k],
            recv_sem=weight_recv.at[w, source],
            device_id={"req": target},
            device_id_type=MESH,
        )

    def own_piece(piece):
        w, own, place = piece
        return pltpu.make_async_copy(own, place(group), own_sem.at[w])

    def send(pieces):
        for piece in pieces:
            for k, target in enumerate((*near, partner)):
                weight_copy(piece, k, target, group).start()

    def arrive(piece, sources):
        for source in sources:
            weight_copy(piece, 0, partner, source).wait_recv()

    def turn(pieces):
        for piece in pieces:
            arrive(piece, near)
            for k in range(len(beside)):
                turn_copy(piece, k).start()
            for k, source in enumerate(near):
                pass_copy(piece, k, source).start()

    def settle(pieces):
        for piece in pieces:
            arrive(piece, diagonal)
            for k, source in enumerate(diagonal):
                pass_copy(piece, len(near) + k, source).start()
        for piece in pieces:
            arrive(piece, (partner, *partner_core))

    def finish(pieces):
        for piece in pieces:
            for k, target in enumerate((*near, partner)):
                weight_copy(piece, k, target, group).wait_send()
            for k, source in enumerate(same_core):
                pass_copy(piece, k, source).wait_send()
            for k in range(len(beside)):
                turn_copy(piece, k).wait_send()

    def cross_copy():
        return pltpu.make_async_remote_copy(
            src_ref=item_shard_ref.at[item_rows(group)],
            dst_ref=items_ref.at[part, item_rows(group)],
            send_sem=cross_send,
            recv_sem=cross_recv,
            device_id={"cand": mate},
            device_id_type=MESH,
        )

    def cross_arrival():
        return pltpu.make_async_remote_copy(
            src_ref=item_shard_ref.at[item_rows(group)],
            dst_ref=items_ref.at[1 - part, item_rows(group)],
            send_sem=cross_send,
            recv_sem=cross_recv,
            device_id={"cand": mate},
            device_id_type=MESH,
        )

    def own_items():
        return pltpu.make_async_copy(item_shard_ref, items_ref.at[part], own_sem.at[0])

    def event_copy(i, k, target, source):
        return pltpu.make_async_remote_copy(
            src_ref=history_ref.at[lax.div(target, lanes) * requests + i],
            dst_ref=events_ref.at[i, events_of(source)],
            send_sem=event_send.at[i, k],
            recv_sem=event_recv.at[i, source],
            device_id={"cand": target},
            device_id_type=MESH,
        )

    def relay_copy(i, k):
        _, source, target = relays[k]
        return pltpu.make_async_remote_copy(
            src_ref=events_ref.at[i, events_of(source)],
            dst_ref=events_ref.at[i, events_of(source)],
            send_sem=event_send.at[i, len(others) + k],
            recv_sem=event_recv.at[i, source],
            device_id={"cand": target},
            device_id_type=MESH,
        )

    def direct(target):
        flag = shard >= 0
        for _, source, end in relays:
            flag = flag & ((shard != source) | (target != end))
        return flag

    def own_event(i):
        return pltpu.make_async_copy(
            history_ref.at[part * requests + i],
            events_ref.at[i, events_of(shard)],
            own_event_sem.at[i],
        )

    def logit_copy(i, k, target, source):
        place = logits_ref.at[lax.rem(source, lanes), lax.div(source, lanes) * requests + i]
        return pltpu.make_async_remote_copy(
            src_ref=place,
            dst_ref=place,
            send_sem=logit_send.at[i, k],
            recv_sem=logit_recv.at[i, source],
            device_id={"cand": target},
            device_id_type=MESH,
        )

    own_items().start()
    for c in range(chunks):
        for piece in chunk_pieces(c):
            own_piece(piece).start()
    for piece in (gate_piece, output_piece, hidden_piece):
        own_piece(piece).start()

    barrier = pltpu.get_barrier_semaphore()
    for target in (*near, partner):
        pl.semaphore_signal(barrier, inc=1, device_id={"req": target}, device_id_type=MESH)
    for target in others:
        pl.semaphore_signal(barrier, inc=1, device_id={"cand": target}, device_id_type=MESH)
    pl.semaphore_wait(barrier, len(near) + 1 + len(others))

    late = {chunks: (gate_piece,), chunks + 1: (output_piece, hidden_piece)}

    def at_level(action, level):
        @pl.when(level < chunks)
        def _():
            action(chunk_pieces(level))

        for edge, pieces in late.items():

            @pl.when(level == edge)
            def _():
                action(pieces)

    def send_events(i):
        for k, target in enumerate(others):

            @pl.when(direct(target))
            def _():
                event_copy(i, k, target, shard).start()

        own_event(i).start()

    send(chunk_pieces(0))
    cross_copy().start()
    send(chunk_pieces(1))

    @pl.loop(0, requests)
    def _(i):
        send_events(i)

    turn(chunk_pieces(0))
    at_level(send, 2)
    cross_arrival().wait_recv()
    send((item_piece,))
    turn(chunk_pieces(1))
    own_items().wait()
    for c in range(chunks):
        for piece in chunk_pieces(c):
            own_piece(piece).wait()
    for piece in (gate_piece, output_piece, hidden_piece):
        own_piece(piece).wait()
    turn((item_piece,))
    settle((item_piece,))

    def enter_chunk(d):
        at_level(send, d + 3)
        settle(chunk_pieces(d))
        query_ref[d] = (
            half_scale
            * silu(
                jnp.dot(
                    items_ref[...].reshape(PARTS * rows, width),
                    query_weight_ref[d],
                    preferred_element_type=jnp.float32,
                )
            )
        ).astype(jnp.bfloat16)

    def relay(i):
        for k, (middle, source, _) in enumerate(relays):

            @pl.when(shard == middle)
            def _():
                event_copy(i, 0, mate, source).wait_recv()
                relay_copy(i, k).start()

    def relayed(source):
        flag = shard < 0
        for middle, start, _ in relays:
            flag = flag | ((shard == middle) & (source == start))
        return flag

    def enter_request(i):
        own_event(i).wait()
        for source in others:

            @pl.when(jnp.logical_not(relayed(source)))
            def _():
                event_copy(i, 0, mate, source).wait_recv()

    def attend(c, r, i):
        length = length_ref[part * requests + i]
        events = events_ref[i]
        pairs_ref[0] = silu(
            jnp.dot(events, key_weight_ref[c], preferred_element_type=jnp.float32)
        ).astype(jnp.bfloat16)
        live = lax.broadcasted_iota(jnp.int32, (history_total, span), 0) < length
        pairs_ref[1] = jnp.where(
            live,
            silu(jnp.dot(events, value_weight_ref[c], preferred_element_type=jnp.float32)),
            0.0,
        ).astype(jnp.bfloat16)
        for h in range(span // head):
            lanes_of = slice(h * head, (h + 1) * head)
            scores = lax.dot_general(
                query_ref[c, :, lanes_of],
                pairs_ref[0, :, lanes_of],
                (((1,), (1,)), ((), ())),
                preferred_element_type=jnp.float32,
            )
            mixed = (scores + scores * jnp.tanh(scores)).astype(jnp.bfloat16)
            attended_ref[r, c, :, lanes_of] = jnp.dot(
                mixed, pairs_ref[1, :, lanes_of], preferred_element_type=jnp.float32
            )

    def run_batch(b):
        @pl.loop(0, chunks * chunks)
        def _(t):
            d = t * 0
            for edge in range(1, chunks):
                d = d + (t >= edge * edge).astype(jnp.int32)
            k = t - d * d
            c = jnp.where(k < d, d, k - d)
            r = jnp.where(k < d, k, d)
            i = b * chunks + r

            @pl.when(k == 0)
            def _():
                relay(b * chunks + d)

            @pl.when((k == 0) & (b == 0))
            def _():
                enter_chunk(d)

            @pl.when((k == d) & (b == 0))
            def _():
                at_level(turn, d + 2)

            @pl.when(k == d)
            def _():
                enter_request(i)

            attend(c, r, i)

        @pl.when(b == 0)
        def _():
            settle((gate_piece,))
            gate_ref[...] = (
                silu(
                    jnp.dot(
                        items_ref[...].reshape(PARTS * rows, width),
                        gate_weight_ref[...],
                        preferred_element_type=jnp.float32,
                    )
                )
                * gain_ref[...]
            )

        @pl.loop(0, chunks)
        def _(r):
            length = jnp.full(
                (1, 1), length_ref[part * requests + b * chunks + r], jnp.int32
            ).astype(jnp.float32)

            @pl.loop(0, PARTS)
            def _(p):
                tile = pl.ds(pl.multiple_of(p * rows, rows), rows)
                attended = jnp.concatenate(
                    [attended_ref[r, c, tile] for c in range(chunks)], axis=-1
                )
                center = attended - jnp.mean(attended, axis=-1, keepdims=True)
                spread = jnp.mean(center * center, axis=-1, keepdims=True)
                normed_ref[r, tile] = (
                    center * lax.rsqrt(spread + EPSILON * length * length) * gate_ref[tile]
                ).astype(jnp.bfloat16)

        @pl.when(b == 0)
        def _():
            settle((output_piece, hidden_piece))

        @pl.loop(0, chunks)
        def _(r):
            i = b * chunks + r
            merged = (
                jnp.dot(normed_ref[r], output_weight_ref[...], preferred_element_type=jnp.float32)
                + items_ref[...].reshape(PARTS * rows, width).astype(jnp.float32)
            ).astype(jnp.bfloat16)
            hidden = silu(
                jnp.dot(merged, hidden_weight_ref[...], preferred_element_type=jnp.float32)
            ).astype(jnp.bfloat16)
            logits = lax.dot_general(
                score_weight_ref[...],
                hidden,
                (((1,), (1,)), ((), ())),
                preferred_element_type=jnp.float32,
            )
            for p in range(PARTS):
                logits_ref[lane, part * requests + i, p] = logits[:, p * rows : (p + 1) * rows]

            for k, target in enumerate(others):
                logit_copy(i, k, target, shard).start()

    if batches == 1:
        run_batch(0)
    else:

        @pl.loop(0, batches)
        def _(b):
            run_batch(b)

    cross_copy().wait_send()
    finish((item_piece, gate_piece, output_piece, hidden_piece))

    @pl.loop(0, chunks)
    def _(c):
        finish(chunk_pieces(c))

    @pl.loop(0, requests)
    def _(i):
        for k, target in enumerate(others):

            @pl.when(direct(target))
            def _():
                event_copy(i, k, target, shard).wait_send()

        for k, (middle, _, _) in enumerate(relays):

            @pl.when(shard == middle)
            def _():
                relay_copy(i, k).wait_send()

        for k, target in enumerate(others):
            logit_copy(i, k, target, shard).wait_send()
            logit_copy(i, k, target, target).wait_recv()


def pair_logits(
    history, length, items, history_weight, candidate_weight, output_weight, hidden_weight, gain,
    score_weight,
):
    all_requests, own_events, width = history.shape
    rows = items.shape[0]
    groups, shards = lax.axis_size("req"), lax.axis_size("cand")
    history_total = own_events * shards
    requests = all_requests // PARTS
    chunks = HEADS // 2
    span = width // chunks
    depth = history_weight.shape[0] * groups
    pieces = 4 + 3 * chunks
    whole = pl.BlockSpec(memory_space=pltpu.VMEM)
    apart = pl.BlockSpec(memory_space=pl.ANY)
    return pl.pallas_call(
        functools.partial(pair_kernel, groups, shards),
        out_shape=jax.ShapeDtypeStruct(
            (shards // PARTS, all_requests, PARTS, score_weight.shape[0], rows), jnp.float32
        ),
        in_specs=[
            pl.BlockSpec(memory_space=pltpu.SMEM),
            apart, apart, apart, apart, apart, apart, whole, whole,
        ],
        out_specs=whole,
        scratch_shapes=[
            pltpu.VMEM((requests, history_total, width), jnp.bfloat16),
            pltpu.VMEM((PARTS, rows, width), jnp.bfloat16),
            pltpu.VMEM((chunks, depth, span), jnp.bfloat16),
            pltpu.VMEM((chunks, depth, span), jnp.bfloat16),
            pltpu.VMEM((chunks, depth, span), jnp.bfloat16),
            pltpu.VMEM((depth, width), jnp.bfloat16),
            pltpu.VMEM((depth, width), jnp.bfloat16),
            pltpu.VMEM((depth, hidden_weight.shape[1]), jnp.bfloat16),
            pltpu.VMEM((chunks, PARTS * rows, span), jnp.bfloat16),
            pltpu.VMEM((PARTS * rows, width), jnp.float32),
            pltpu.VMEM((2, history_total, span), jnp.bfloat16),
            pltpu.VMEM((chunks, chunks, PARTS * rows, span), jnp.float32),
            pltpu.VMEM((chunks, PARTS * rows, width), jnp.bfloat16),
            pltpu.SemaphoreType.DMA((pieces, groups // 2)),
            pltpu.SemaphoreType.DMA((pieces, groups)),
            pltpu.SemaphoreType.DMA((pieces, groups // 2)),
            pltpu.SemaphoreType.DMA((pieces, groups // 2)),
            pltpu.SemaphoreType.DMA,
            pltpu.SemaphoreType.DMA,
            pltpu.SemaphoreType.DMA((requests, shards + 1)),
            pltpu.SemaphoreType.DMA((requests, shards)),
            pltpu.SemaphoreType.DMA((requests, shards)),
            pltpu.SemaphoreType.DMA((requests, shards)),
            pltpu.SemaphoreType.DMA((pieces,)),
            pltpu.SemaphoreType.DMA((requests,)),
        ],
        compiler_params=pltpu.CompilerParams(
            collective_id=0, has_side_effects=True, vmem_limit_bytes=60 * 1024 * 1024
        ),
    )(
        length, history, items, history_weight, candidate_weight, output_weight, hidden_weight,
        gain, score_weight,
    )


def blend(logits, candidate_count, block_shard, block_index, item_ages, item_blocks):
    shards = lax.axis_size("cand")
    mine = lax.axis_index("cand")
    lanes = shards // PARTS
    requests, max_blocks = block_shard.shape
    per_scorer = max_blocks // shards
    logits = logits.reshape(lanes, requests, PARTS, -1, item_blocks, BLOCK)
    ids = lax.dynamic_slice_in_dim(
        block_shard * item_blocks + block_index, mine * per_scorer, per_scorer, 1
    )
    names = (
        jnp.arange(shards * item_blocks, dtype=jnp.int32)
        .reshape(PARTS, lanes, item_blocks)
        .transpose(1, 0, 2)[:, None, :, None, :, None]
    )
    picked = ids[None, :, None, :, None, None] == names
    first, second = (
        jnp.sum(jnp.where(picked, logits[:, :, :, None, c], 0.0), axis=(0, 2, 4)) for c in (0, 1)
    )
    decays = jnp.exp(
        -item_ages.astype(jnp.float32).reshape(requests, per_scorer, BLOCK) / AGE_SCALE
    )
    blended = decays * first + (1.0 - decays) * second
    row_number = (mine * per_scorer + jnp.arange(per_scorer, dtype=jnp.int32))[
        None, :, None
    ] * BLOCK + jnp.arange(BLOCK, dtype=jnp.int32)[None, None, :]
    kept_rows = row_number < candidate_count[:, None, None]
    return jnp.where(kept_rows, blended, 0.0).reshape(requests, per_scorer * BLOCK)


def local(
    history,
    history_length,
    candidate_count,
    block_shard,
    block_index,
    item_table,
    item_ages,
    history_weight,
    candidate_weight,
    output_weight,
    hidden_weight,
    norm_gain,
    score_weight,
):
    item_blocks = item_table.shape[0]
    logits = pair_logits(
        history,
        history_length,
        item_table.reshape(-1, item_table.shape[2]),
        history_weight,
        candidate_weight,
        output_weight,
        hidden_weight,
        norm_gain[None, :],
        score_weight,
    )
    return blend(logits, candidate_count, block_shard, block_index, item_ages, item_blocks)


def solution(mesh):
    return jax.shard_map(
        local,
        mesh=mesh,
        in_specs=(
            P("req", "cand", None),
            P("req"),
            P("req"),
            P("req", None),
            P("req", None),
            P("cand", None, None),
            P("req", "cand"),
            P("req", None),
            P("req", None),
            P("req", None),
            P("req", None),
            P(),
            P(),
        ),
        out_specs=P("req", "cand"),
        check_vma=False,
    )
```

```python
import functools
import math

import jax
import jax.numpy as jnp
from jax import lax
from jax.experimental import pallas as pl
from jax.experimental.pallas import tpu as pltpu
from jax.sharding import PartitionSpec as P

HEADS = 8
BLOCK = 128
EPSILON = 1e-05
AGE_SCALE = 48.0
PARTS = 2
LOGIT_SENDS = 2


def silu(value):
    half = 0.5 * value
    return half + half * jnp.tanh(half)


MESH = pl.DeviceIdType.MESH


def pair_kernel(
    groups,
    shards,
    length_ref,
    count_ref,
    block_shard_ref,
    block_index_ref,
    history_ref,
    item_shard_ref,
    history_shard_ref,
    candidate_shard_ref,
    output_shard_ref,
    hidden_shard_ref,
    ages_ref,
    gain_ref,
    score_weight_ref,
    scores_ref,
    events_ref,
    items_ref,
    chunk_weight_ref,
    gate_weight_ref,
    last_weight_ref,
    query_ref,
    gate_ref,
    pairs_ref,
    attended_ref,
    normed_ref,
    logits_ref,
    decay_ref,
    limit_ref,
    picked_ref,
    weight_send,
    weight_recv,
    pass_send,
    turn_send,
    cross_send,
    cross_recv,
    event_send,
    event_recv,
    logit_send,
    logit_recv,
    own_sem,
    own_event_sem,
):
    group = lax.axis_index("req")
    shard = lax.axis_index("cand")
    partner = group + 1 - 2 * lax.rem(group, 2)
    own_events = history_ref.shape[1]
    width = history_ref.shape[2]
    lanes = shards // PARTS
    part, lane = lax.div(shard, lanes), lax.rem(shard, lanes)
    mate = lax.rem(shard + lanes, shards)
    requests, history_total = events_ref.shape[:2]
    chunks, _, span = query_ref.shape
    batch_sends = chunks // LOGIT_SENDS
    batches = requests // chunks
    rows = item_shard_ref.shape[0]
    head = width // HEADS
    half_scale = 0.5 / math.sqrt(head)
    depth = history_shard_ref.shape[0]
    item_depth = rows // groups
    half = groups // 2
    row, core = lax.div(group, half), lax.rem(group, 2)
    across = lax.rem(group + half, groups)
    beside = [row * half + lax.rem(group - row * half + 2 * d, half) for d in range(1, half // 2)]
    diagonal = [lax.rem(source + half, groups) for source in beside]
    near = (*beside, across)
    same_core = (*near, *diagonal)
    partner_core = [source + partner - group for source in same_core]
    others = [lax.rem(shard + d, shards) for d in range(1, shards)]
    relays = ((1, 2, 0), (2, 1, 3)) if shards == 4 else ()

    def rows_of(source):
        return pl.ds(pl.multiple_of(source * depth, depth), depth)

    def item_rows(source):
        return pl.ds(pl.multiple_of(source * item_depth, item_depth), item_depth)

    def events_of(source):
        return pl.ds(pl.multiple_of(source * own_events, own_events), own_events)

    def columns(start):
        return pl.ds(pl.multiple_of(start, span), span)

    item_piece = (0, lambda source: items_ref.at[1 - part, item_rows(source)])
    gate_piece = (1, lambda source: gate_weight_ref.at[rows_of(source)])
    last_piece = (2, lambda source: last_weight_ref.at[rows_of(source)])

    def chunk_piece(c):
        return (3 + c, lambda source: chunk_weight_ref.at[c, rows_of(source)])

    def weight_copy(piece, k, target, source):
        w, place = piece
        return pltpu.make_async_remote_copy(
            src_ref=place(source),
            dst_ref=place(source),
            send_sem=weight_send.at[w, k],
            recv_sem=weight_recv.at[w, source],
            device_id={"req": target},
            device_id_type=MESH,
        )

    def pass_copy(piece, k, source):
        w, place = piece
        return pltpu.make_async_remote_copy(
            src_ref=place(source),
            dst_ref=place(source),
            send_sem=pass_send.at[w, k],
            recv_sem=weight_recv.at[w, source],
            device_id={"req": partner},
            device_id_type=MESH,
        )

    def turn_copy(piece, k):
        w, place = piece
        source = beside[k] + core * (across - beside[k])
        target = across + core * (beside[k] - across)
        return pltpu.make_async_remote_copy(
            src_ref=place(source),
            dst_ref=place(source),
            send_sem=turn_send.at[w, k],
            recv_sem=weight_recv.at[w, source],
            device_id={"req": target},
            device_id_type=MESH,
        )

    def own_parts():
        own = rows_of(group)
        parts = [(item_shard_ref, items_ref.at[part])]
        for c in range(chunks):
            for k, (shard_ref, start) in enumerate(
                ((candidate_shard_ref, 0), (history_shard_ref, 0), (history_shard_ref, width))
            ):
                parts.append(
                    (
                        shard_ref.at[:, pl.ds(start + c * span, span)],
                        chunk_weight_ref.at[c, own, pl.ds(k * span, span)],
                    )
                )
        parts.append((candidate_shard_ref.at[:, pl.ds(width, width)], gate_weight_ref.at[own]))
        parts.append((output_shard_ref, last_weight_ref.at[own, pl.ds(0, width)]))
        parts.append(
            (hidden_shard_ref, last_weight_ref.at[own, pl.ds(width, hidden_shard_ref.shape[1])])
        )
        return [
            pltpu.make_async_copy(source, target, own_sem.at[k])
            for k, (source, target) in enumerate(parts)
        ]

    def send(pieces):
        for piece in pieces:
            for k, target in enumerate((*near, partner)):
                weight_copy(piece, k, target, group).start()

    def arrive(piece, sources):
        for source in sources:
            weight_copy(piece, 0, partner, source).wait_recv()

    def turn(pieces):
        for piece in pieces:
            arrive(piece, near)
            for k in range(len(beside)):
                turn_copy(piece, k).start()
            for k, source in enumerate(near):
                pass_copy(piece, k, source).start()

    def settle(pieces):
        for piece in pieces:
            arrive(piece, diagonal)
            for k, source in enumerate(diagonal):
                pass_copy(piece, len(near) + k, source).start()
        for piece in pieces:
            arrive(piece, (partner, *partner_core))

    def finish(pieces):
        for piece in pieces:
            for k, target in enumerate((*near, partner)):
                weight_copy(piece, k, target, group).wait_send()
            for k, source in enumerate(same_core):
                pass_copy(piece, k, source).wait_send()
            for k in range(len(beside)):
                turn_copy(piece, k).wait_send()

    def cross_copy():
        return pltpu.make_async_remote_copy(
            src_ref=item_shard_ref.at[item_rows(group)],
            dst_ref=items_ref.at[part, item_rows(group)],
            send_sem=cross_send,
            recv_sem=cross_recv,
            device_id={"cand": mate},
            device_id_type=MESH,
        )

    def cross_arrival():
        return pltpu.make_async_remote_copy(
            src_ref=item_shard_ref.at[item_rows(group)],
            dst_ref=items_ref.at[1 - part, item_rows(group)],
            send_sem=cross_send,
            recv_sem=cross_recv,
            device_id={"cand": mate},
            device_id_type=MESH,
        )

    def event_copy(i, k, target, source):
        return pltpu.make_async_remote_copy(
            src_ref=history_ref.at[lax.div(target, lanes) * requests + i],
            dst_ref=events_ref.at[i, events_of(source)],
            send_sem=event_send.at[i, k],
            recv_sem=event_recv.at[i, source],
            device_id={"cand": target},
            device_id_type=MESH,
        )

    def relay_copy(i, k):
        _, source, target = relays[k]
        return pltpu.make_async_remote_copy(
            src_ref=events_ref.at[i, events_of(source)],
            dst_ref=events_ref.at[i, events_of(source)],
            send_sem=event_send.at[i, len(others) + k],
            recv_sem=event_recv.at[i, source],
            device_id={"cand": target},
            device_id_type=MESH,
        )

    def direct(target):
        flag = shard >= 0
        for _, source, end in relays:
            flag = flag & ((shard != source) | (target != end))
        return flag

    def own_event(i):
        return pltpu.make_async_copy(
            history_ref.at[part * requests + i],
            events_ref.at[i, events_of(shard)],
            own_event_sem.at[i],
        )

    def logit_copy(first, k, target, source):
        place = logits_ref.at[
            lax.rem(source, lanes), pl.ds(lax.div(source, lanes) * requests + first, batch_sends)
        ]
        step = lax.div(first, batch_sends)
        return pltpu.make_async_remote_copy(
            src_ref=place,
            dst_ref=place,
            send_sem=logit_send.at[step, k],
            recv_sem=logit_recv.at[step, source],
            device_id={"cand": target},
            device_id_type=MESH,
        )

    own = own_parts()
    for copy in own:
        copy.start()

    barrier = pltpu.get_barrier_semaphore()
    for target in (*near, partner):
        pl.semaphore_signal(barrier, inc=1, device_id={"req": target}, device_id_type=MESH)
    for target in others:
        pl.semaphore_signal(barrier, inc=1, device_id={"cand": target}, device_id_type=MESH)
    pl.semaphore_wait(barrier, len(near) + 1 + len(others))

    late = {chunks: gate_piece, chunks + 1: last_piece}

    def at_level(action, level):
        @pl.when(level < chunks)
        def _():
            action((chunk_piece(level),))

        for edge, piece in late.items():

            @pl.when(level == edge)
            def _():
                action((piece,))

    def send_events(i):
        for k, target in enumerate(others):

            @pl.when(direct(target))
            def _():
                event_copy(i, k, target, shard).start()

        own_event(i).start()

    for copy in own:
        copy.wait()
    send((chunk_piece(0),))
    cross_copy().start()
    send((chunk_piece(1),))

    @pl.loop(0, requests)
    def _(i):
        send_events(i)

    decay_ref[...] = jnp.exp(-ages_ref[...].astype(jnp.float32) / AGE_SCALE)

    for q in range(count_ref.shape[0]):
        limit_ref[q : q + 1] = jnp.full((1, limit_ref.shape[1]), count_ref[q], jnp.int32)

    turn((chunk_piece(0),))
    cross_arrival().wait_recv()
    send((item_piece,))
    at_level(send, 2)
    turn((chunk_piece(1),))
    turn((item_piece,))
    settle((item_piece,))

    def enter_chunk(d):
        at_level(send, d + 3)
        settle((chunk_piece(d),))
        query_ref[d] = (
            half_scale
            * silu(
                jnp.dot(
                    items_ref[...].reshape(PARTS * rows, width),
                    chunk_weight_ref[d, :, :span],
                    preferred_element_type=jnp.float32,
                )
            )
        ).astype(jnp.bfloat16)

    def relay(i):
        for k, (middle, source, _) in enumerate(relays):

            @pl.when(shard == middle)
            def _():
                event_copy(i, 0, mate, source).wait_recv()
                relay_copy(i, k).start()

    def relayed(source):
        flag = shard < 0
        for middle, start, _ in relays:
            flag = flag | ((shard == middle) & (source == start))
        return flag

    def enter_request(i):
        own_event(i).wait()
        for source in others:

            @pl.when(jnp.logical_not(relayed(source)))
            def _():
                event_copy(i, 0, mate, source).wait_recv()

    def attend(c, r, i):
        length = length_ref[part * requests + i]
        events = events_ref[i]
        pairs_ref[0] = silu(
            jnp.dot(
                events,
                chunk_weight_ref[c, :, span : 2 * span],
                preferred_element_type=jnp.float32,
            )
        ).astype(jnp.bfloat16)
        live = lax.broadcasted_iota(jnp.int32, (history_total, span), 0) < length
        pairs_ref[1] = jnp.where(
            live,
            silu(
                jnp.dot(
                    events,
                    chunk_weight_ref[c, :, 2 * span :],
                    preferred_element_type=jnp.float32,
                )
            ),
            0.0,
        ).astype(jnp.bfloat16)
        heads = [slice(h * head, (h + 1) * head) for h in range(span // head)]
        scores = [
            lax.dot_general(
                query_ref[c, :, h],
                pairs_ref[0, :, h],
                (((1,), (1,)), ((), ())),
                preferred_element_type=jnp.float32,
            )
            for h in heads
        ]
        mixed = [(value + value * jnp.tanh(value)).astype(jnp.bfloat16) for value in scores]
        for h, value in zip(heads, mixed):
            attended_ref[r, c, :, h] = jnp.dot(
                value, pairs_ref[1, :, h], preferred_element_type=jnp.float32
            )

    def run_batch(b):
        @pl.loop(0, chunks * chunks)
        def _(t):
            d = t * 0
            for edge in range(1, chunks):
                d = d + (t >= edge * edge).astype(jnp.int32)
            k = t - d * d
            c = jnp.where(k < d, d, k - d)
            r = jnp.where(k < d, k, d)
            i = b * chunks + r

            @pl.when(k == 0)
            def _():
                relay(b * chunks + d)

            @pl.when((k == 0) & (b == 0))
            def _():
                enter_chunk(d)

            @pl.when((k == d) & (b == 0))
            def _():
                at_level(turn, d + 2)

            @pl.when(k == d)
            def _():
                enter_request(i)

            attend(c, r, i)

        @pl.when(b == 0)
        def _():
            settle((gate_piece,))
            gate_ref[...] = (
                silu(
                    jnp.dot(
                        items_ref[...].reshape(PARTS * rows, width),
                        gate_weight_ref[...],
                        preferred_element_type=jnp.float32,
                    )
                )
                * gain_ref[...]
            )

        @pl.loop(0, chunks)
        def _(r):
            length = jnp.full(
                (1, 1), length_ref[part * requests + b * chunks + r], jnp.int32
            ).astype(jnp.float32)

            @pl.loop(0, PARTS)
            def _(p):
                tile = pl.ds(pl.multiple_of(p * rows, rows), rows)
                attended = jnp.concatenate(
                    [attended_ref[r, c, tile] for c in range(chunks)], axis=-1
                )
                center = attended - jnp.mean(attended, axis=-1, keepdims=True)
                spread = jnp.mean(center * center, axis=-1, keepdims=True)
                normed_ref[r, tile] = (
                    center * lax.rsqrt(spread + EPSILON * length * length) * gate_ref[tile]
                ).astype(jnp.bfloat16)

        @pl.when(b == 0)
        def _():
            settle((last_piece,))

        @pl.loop(0, chunks)
        def _(r):
            i = b * chunks + r
            merged = (
                jnp.dot(normed_ref[r], last_weight_ref[:, :width], preferred_element_type=jnp.float32)
                + items_ref[...].reshape(PARTS * rows, width).astype(jnp.float32)
            ).astype(jnp.bfloat16)
            hidden = silu(
                jnp.dot(merged, last_weight_ref[:, width:], preferred_element_type=jnp.float32)
            ).astype(jnp.bfloat16)
            logits = lax.dot_general(
                score_weight_ref[...],
                hidden,
                (((1,), (1,)), ((), ())),
                preferred_element_type=jnp.float32,
            )
            for n in range(PARTS * rows // BLOCK):
                logits_ref[lane, part * requests + i, n // (rows // BLOCK), n % (rows // BLOCK)] = (
                    logits[:, n * BLOCK : (n + 1) * BLOCK]
                )

            @pl.when(lax.rem(r, batch_sends) == batch_sends - 1)
            def _():
                for k, target in enumerate(others):
                    logit_copy(i + 1 - batch_sends, k, target, shard).start()

    if batches == 1:
        run_batch(0)
    else:

        @pl.loop(0, batches)
        def _(b):
            run_batch(b)

    cross_copy().wait_send()
    finish((item_piece, gate_piece, last_piece))

    @pl.loop(0, chunks)
    def _(c):
        finish((chunk_piece(c),))

    @pl.loop(0, requests)
    def _(i):
        for k, target in enumerate(others):

            @pl.when(direct(target))
            def _():
                event_copy(i, k, target, shard).wait_send()

        for k, (middle, _, _) in enumerate(relays):

            @pl.when(shard == middle)
            def _():
                relay_copy(i, k).wait_send()

    @pl.loop(0, requests // batch_sends)
    def _(step):
        for k, target in enumerate(others):
            logit_copy(step * batch_sends, k, target, shard).wait_send()
            logit_copy(step * batch_sends, k, target, target).wait_recv()

    all_requests, max_blocks = block_shard_ref.shape
    per_scorer = max_blocks // shards

    for q in range(all_requests):
        for j in range(per_scorer):
            slot = shard * per_scorer + j
            source = block_shard_ref[q, slot]
            found = logits_ref[
                lax.rem(source, lanes), q, lax.div(source, lanes), block_index_ref[q, slot]
            ]
            for n in range(score_weight_ref.shape[0]):
                picked_ref[n, q : q + 1, j * BLOCK : (j + 1) * BLOCK] = found[n : n + 1]

    row_number = shard * (per_scorer * BLOCK) + lax.broadcasted_iota(jnp.int32, ages_ref.shape, 1)
    decay = decay_ref[...]
    blended = decay * picked_ref[0] + (1.0 - decay) * picked_ref[1]
    scores_ref[...] = jnp.where(row_number < limit_ref[...], blended, 0.0)


def pair_scores(
    length, count, block_shard, block_index, history, items, history_weight, candidate_weight,
    output_weight, hidden_weight, ages, gain, score_weight,
):
    all_requests, own_events, width = history.shape
    rows = items.shape[0]
    groups, shards = lax.axis_size("req"), lax.axis_size("cand")
    history_total = own_events * shards
    requests = all_requests // PARTS
    chunks = HEADS // 2
    span = width // chunks
    depth = history_weight.shape[0] * groups
    pieces = 3 + chunks
    small = pl.BlockSpec(memory_space=pltpu.SMEM)
    whole = pl.BlockSpec(memory_space=pltpu.VMEM)
    apart = pl.BlockSpec(memory_space=pl.ANY)
    sends = requests * LOGIT_SENDS // chunks
    return pl.pallas_call(
        functools.partial(pair_kernel, groups, shards),
        out_shape=jax.ShapeDtypeStruct(ages.shape, jnp.float32),
        in_specs=[small] * 4 + [apart] * 6 + [whole] * 3,
        out_specs=whole,
        scratch_shapes=[
            pltpu.VMEM((requests, history_total, width), jnp.bfloat16),
            pltpu.VMEM((PARTS, rows, width), jnp.bfloat16),
            pltpu.VMEM((chunks, depth, 3 * span), jnp.bfloat16),
            pltpu.VMEM((depth, width), jnp.bfloat16),
            pltpu.VMEM((depth, width + hidden_weight.shape[1]), jnp.bfloat16),
            pltpu.VMEM((chunks, PARTS * rows, span), jnp.bfloat16),
            pltpu.VMEM((PARTS * rows, width), jnp.float32),
            pltpu.VMEM((2, history_total, span), jnp.bfloat16),
            pltpu.VMEM((chunks, chunks, PARTS * rows, span), jnp.float32),
            pltpu.VMEM((chunks, PARTS * rows, width), jnp.bfloat16),
            pltpu.VMEM(
                (
                    shards // PARTS, all_requests, PARTS, rows // BLOCK, score_weight.shape[0],
                    BLOCK,
                ),
                jnp.float32,
            ),
            pltpu.VMEM(ages.shape, jnp.float32),
            pltpu.VMEM(ages.shape, jnp.int32),
            pltpu.VMEM((score_weight.shape[0], *ages.shape), jnp.float32),
            pltpu.SemaphoreType.DMA((pieces, groups // 2)),
            pltpu.SemaphoreType.DMA((pieces, groups)),
            pltpu.SemaphoreType.DMA((pieces, groups // 2)),
            pltpu.SemaphoreType.DMA((pieces, groups // 2)),
            pltpu.SemaphoreType.DMA,
            pltpu.SemaphoreType.DMA,
            pltpu.SemaphoreType.DMA((requests, shards + 1)),
            pltpu.SemaphoreType.DMA((requests, shards)),
            pltpu.SemaphoreType.DMA((sends, shards)),
            pltpu.SemaphoreType.DMA((sends, shards)),
            pltpu.SemaphoreType.DMA((4 + 3 * chunks,)),
            pltpu.SemaphoreType.DMA((requests,)),
        ],
        compiler_params=pltpu.CompilerParams(
            collective_id=0, has_side_effects=True, vmem_limit_bytes=60 * 1024 * 1024
        ),
    )(
        length, count, block_shard, block_index, history, items, history_weight, candidate_weight,
        output_weight, hidden_weight, ages, gain, score_weight,
    )


def local(
    history,
    history_length,
    candidate_count,
    block_shard,
    block_index,
    item_table,
    item_ages,
    history_weight,
    candidate_weight,
    output_weight,
    hidden_weight,
    norm_gain,
    score_weight,
):
    return pair_scores(
        history_length,
        candidate_count,
        block_shard,
        block_index,
        history,
        item_table.reshape(-1, item_table.shape[2]),
        history_weight,
        candidate_weight,
        output_weight,
        hidden_weight,
        item_ages,
        norm_gain[None, :],
        score_weight,
    )


def solution(mesh):
    return jax.shard_map(
        local,
        mesh=mesh,
        in_specs=(
            P("req", "cand", None),
            P("req"),
            P("req"),
            P("req", None),
            P("req", None),
            P("cand", None, None),
            P("req", "cand"),
            P("req", None),
            P("req", None),
            P("req", None),
            P("req", None),
            P(),
            P(),
        ),
        out_specs=P("req", "cand"),
        check_vma=False,
    )
```

```python
import functools
import math

import jax
import jax.numpy as jnp
from jax import lax
from jax.experimental import pallas as pl
from jax.experimental.pallas import tpu as pltpu
from jax.sharding import PartitionSpec as P

HEADS = 8
BLOCK = 128
EPSILON = 1e-05
AGE_SCALE = 48.0
PARTS = 2
LOGIT_SENDS = 2
ENTER = {1: [('send', 4)], 2: [('send', 5)]}
MIDDLE = {0: [('hand', 1), ('turn', 2)], 1: [('hand', 2), ('turn', 3)], 2: [('hand', 3), ('turn', 4)], 3: [('hand', 4), ('turn', 5)]}


def silu(value):
    half = 0.5 * value
    return half + half * jnp.tanh(half)


MESH = pl.DeviceIdType.MESH


def pair_kernel(
    groups,
    shards,
    length_ref,
    count_ref,
    block_shard_ref,
    block_index_ref,
    history_ref,
    item_shard_ref,
    history_shard_ref,
    candidate_shard_ref,
    output_shard_ref,
    hidden_shard_ref,
    ages_ref,
    gain_ref,
    score_weight_ref,
    scores_ref,
    events_ref,
    items_ref,
    chunk_weight_ref,
    gate_weight_ref,
    last_weight_ref,
    query_ref,
    gate_ref,
    pairs_ref,
    attended_ref,
    normed_ref,
    logits_ref,
    decay_ref,
    limit_ref,
    picked_ref,
    weight_send,
    weight_recv,
    pass_send,
    turn_send,
    cross_send,
    cross_recv,
    event_send,
    event_recv,
    logit_send,
    logit_recv,
    own_sem,
    own_event_sem,
):
    group = lax.axis_index("req")
    shard = lax.axis_index("cand")
    partner = group + 1 - 2 * lax.rem(group, 2)
    own_events = history_ref.shape[1]
    width = history_ref.shape[2]
    lanes = shards // PARTS
    part, lane = lax.div(shard, lanes), lax.rem(shard, lanes)
    mate = lax.rem(shard + lanes, shards)
    requests, history_total = events_ref.shape[:2]
    chunks, _, span = query_ref.shape
    batch_sends = chunks // LOGIT_SENDS
    batches = requests // chunks
    rows = item_shard_ref.shape[0]
    head = width // HEADS
    half_scale = 0.5 / math.sqrt(head)
    depth = history_shard_ref.shape[0]
    item_depth = rows // groups
    half = groups // 2
    row, core = lax.div(group, half), lax.rem(group, 2)
    across = lax.rem(group + half, groups)
    beside = [row * half + lax.rem(group - row * half + 2 * d, half) for d in range(1, half // 2)]
    diagonal = [lax.rem(source + half, groups) for source in beside]
    near = (*beside, across)
    same_core = (*near, *diagonal)
    partner_core = [source + partner - group for source in same_core]
    others = [lax.rem(shard + d, shards) for d in range(1, shards)]
    relays = ((1, 2, 0), (2, 1, 3)) if shards == 4 else ()

    def rows_of(source):
        return pl.ds(pl.multiple_of(source * depth, depth), depth)

    def item_rows(source):
        return pl.ds(pl.multiple_of(source * item_depth, item_depth), item_depth)

    def events_of(source):
        return pl.ds(pl.multiple_of(source * own_events, own_events), own_events)

    def columns(start):
        return pl.ds(pl.multiple_of(start, span), span)

    item_piece = (0, lambda source: items_ref.at[1 - part, item_rows(source)])
    gate_piece = (1, lambda source: gate_weight_ref.at[rows_of(source)])
    last_piece = (2, lambda source: last_weight_ref.at[rows_of(source)])

    def chunk_piece(c):
        return (3 + c, lambda source: chunk_weight_ref.at[c, rows_of(source)])

    def weight_copy(piece, k, target, source):
        w, place = piece
        return pltpu.make_async_remote_copy(
            src_ref=place(source),
            dst_ref=place(source),
            send_sem=weight_send.at[w, k],
            recv_sem=weight_recv.at[w, source],
            device_id={"req": target},
            device_id_type=MESH,
        )

    def pass_copy(piece, k, source):
        w, place = piece
        return pltpu.make_async_remote_copy(
            src_ref=place(source),
            dst_ref=place(source),
            send_sem=pass_send.at[w, k],
            recv_sem=weight_recv.at[w, source],
            device_id={"req": partner},
            device_id_type=MESH,
        )

    def turn_copy(piece, k):
        w, place = piece
        source = beside[k] + core * (across - beside[k])
        target = across + core * (beside[k] - across)
        return pltpu.make_async_remote_copy(
            src_ref=place(source),
            dst_ref=place(source),
            send_sem=turn_send.at[w, k],
            recv_sem=weight_recv.at[w, source],
            device_id={"req": target},
            device_id_type=MESH,
        )

    def own_parts():
        own = rows_of(group)
        parts = [(item_shard_ref, items_ref.at[part])]
        for c in range(chunks):
            for k, (shard_ref, start) in enumerate(
                ((candidate_shard_ref, 0), (history_shard_ref, 0), (history_shard_ref, width))
            ):
                parts.append(
                    (
                        shard_ref.at[:, pl.ds(start + c * span, span)],
                        chunk_weight_ref.at[c, own, pl.ds(k * span, span)],
                    )
                )
        parts.append((candidate_shard_ref.at[:, pl.ds(width, width)], gate_weight_ref.at[own]))
        parts.append((output_shard_ref, last_weight_ref.at[own, pl.ds(0, width)]))
        parts.append(
            (hidden_shard_ref, last_weight_ref.at[own, pl.ds(width, hidden_shard_ref.shape[1])])
        )
        return [
            pltpu.make_async_copy(source, target, own_sem.at[k])
            for k, (source, target) in enumerate(parts)
        ]

    def send(pieces):
        for piece in pieces:
            for k, target in enumerate((*near, partner)):
                weight_copy(piece, k, target, group).start()

    def arrive(piece, sources):
        for source in sources:
            weight_copy(piece, 0, partner, source).wait_recv()

    def turn(pieces):
        for piece in pieces:
            arrive(piece, near)
            for k in range(len(beside)):
                turn_copy(piece, k).start()
            for k, source in enumerate(near):
                pass_copy(piece, k, source).start()

    def hand(pieces):
        for piece in pieces:
            arrive(piece, diagonal)
            for k, source in enumerate(diagonal):
                pass_copy(piece, len(near) + k, source).start()

    def collect(pieces):
        for piece in pieces:
            arrive(piece, (partner, *partner_core))

    def finish(pieces):
        for piece in pieces:
            for k, target in enumerate((*near, partner)):
                weight_copy(piece, k, target, group).wait_send()
            for k, source in enumerate(same_core):
                pass_copy(piece, k, source).wait_send()
            for k in range(len(beside)):
                turn_copy(piece, k).wait_send()

    def cross_copy():
        return pltpu.make_async_remote_copy(
            src_ref=item_shard_ref.at[item_rows(group)],
            dst_ref=items_ref.at[part, item_rows(group)],
            send_sem=cross_send,
            recv_sem=cross_recv,
            device_id={"cand": mate},
            device_id_type=MESH,
        )

    def cross_arrival():
        return pltpu.make_async_remote_copy(
            src_ref=item_shard_ref.at[item_rows(group)],
            dst_ref=items_ref.at[1 - part, item_rows(group)],
            send_sem=cross_send,
            recv_sem=cross_recv,
            device_id={"cand": mate},
            device_id_type=MESH,
        )

    def event_copy(i, k, target, source):
        return pltpu.make_async_remote_copy(
            src_ref=history_ref.at[lax.div(target, lanes) * requests + i],
            dst_ref=events_ref.at[i, events_of(source)],
            send_sem=event_send.at[i, k],
            recv_sem=event_recv.at[i, source],
            device_id={"cand": target},
            device_id_type=MESH,
        )

    def relay_copy(i, k):
        _, source, target = relays[k]
        return pltpu.make_async_remote_copy(
            src_ref=events_ref.at[i, events_of(source)],
            dst_ref=events_ref.at[i, events_of(source)],
            send_sem=event_send.at[i, len(others) + k],
            recv_sem=event_recv.at[i, source],
            device_id={"cand": target},
            device_id_type=MESH,
        )

    def direct(target):
        flag = shard >= 0
        for _, source, end in relays:
            flag = flag & ((shard != source) | (target != end))
        return flag

    def own_event(i):
        return pltpu.make_async_copy(
            history_ref.at[part * requests + i],
            events_ref.at[i, events_of(shard)],
            own_event_sem.at[i],
        )

    def logit_copy(first, k, target, source):
        place = logits_ref.at[
            lax.rem(source, lanes), pl.ds(lax.div(source, lanes) * requests + first, batch_sends)
        ]
        step = lax.div(first, batch_sends)
        return pltpu.make_async_remote_copy(
            src_ref=place,
            dst_ref=place,
            send_sem=logit_send.at[step, k],
            recv_sem=logit_recv.at[step, source],
            device_id={"cand": target},
            device_id_type=MESH,
        )

    own = own_parts()
    for copy in own:
        copy.start()

    barrier = pltpu.get_barrier_semaphore()
    for target in (*near, partner):
        pl.semaphore_signal(barrier, inc=1, device_id={"req": target}, device_id_type=MESH)
    for target in others:
        pl.semaphore_signal(barrier, inc=1, device_id={"cand": target}, device_id_type=MESH)
    pl.semaphore_wait(barrier, len(near) + 1 + len(others))

    late = {-1: item_piece, chunks: gate_piece, chunks + 1: last_piece}

    def piece_at(level):
        return late[level] if level in late else chunk_piece(level)

    def run_steps(steps):
        for action, level in steps:
            {"send": send, "turn": turn, "hand": hand}[action]((piece_at(level),))

    def at_chunk(table, d):
        for edge, steps in table.items():

            @pl.when(d == edge)
            def _():
                run_steps(steps)

    def send_events(i):
        for k, target in enumerate(others):

            @pl.when(direct(target))
            def _():
                event_copy(i, k, target, shard).start()

        own_event(i).start()

    for copy in own:
        copy.wait()
    send((chunk_piece(0),))
    cross_copy().start()
    send((chunk_piece(1),))

    @pl.loop(0, requests)
    def _(i):
        send_events(i)

    decay_ref[...] = jnp.exp(-ages_ref[...].astype(jnp.float32) / AGE_SCALE)
    for q in range(count_ref.shape[0]):
        limit_ref[q : q + 1] = jnp.full((1, limit_ref.shape[1]), count_ref[q], jnp.int32)
    turn((chunk_piece(0),))
    cross_arrival().wait_recv()
    send((item_piece,))
    send((chunk_piece(2),))
    turn((chunk_piece(1),))
    hand((chunk_piece(0),))
    turn((item_piece,))
    hand((item_piece,))
    send((chunk_piece(3),))
    collect((item_piece,))

    def enter_chunk(d):
        at_chunk(ENTER, d)
        collect((chunk_piece(d),))
        query_ref[d] = (
            half_scale
            * silu(
                jnp.dot(
                    items_ref[...].reshape(PARTS * rows, width),
                    chunk_weight_ref[d, :, :span],
                    preferred_element_type=jnp.float32,
                )
            )
        ).astype(jnp.bfloat16)

    def relay(i):
        for k, (middle, source, _) in enumerate(relays):

            @pl.when(shard == middle)
            def _():
                event_copy(i, 0, mate, source).wait_recv()
                relay_copy(i, k).start()

    def relayed(source):
        flag = shard < 0
        for middle, start, _ in relays:
            flag = flag | ((shard == middle) & (source == start))
        return flag

    def enter_request(i):
        own_event(i).wait()
        for source in others:

            @pl.when(jnp.logical_not(relayed(source)))
            def _():
                event_copy(i, 0, mate, source).wait_recv()

    def attend(c, r, i):
        length = length_ref[part * requests + i]
        events = events_ref[i]
        pairs_ref[0] = silu(
            jnp.dot(
                events,
                chunk_weight_ref[c, :, span : 2 * span],
                preferred_element_type=jnp.float32,
            )
        ).astype(jnp.bfloat16)
        live = lax.broadcasted_iota(jnp.int32, (history_total, span), 0) < length
        pairs_ref[1] = jnp.where(
            live,
            silu(
                jnp.dot(
                    events,
                    chunk_weight_ref[c, :, 2 * span :],
                    preferred_element_type=jnp.float32,
                )
            ),
            0.0,
        ).astype(jnp.bfloat16)
        heads = [slice(h * head, (h + 1) * head) for h in range(span // head)]
        scores = [
            lax.dot_general(
                query_ref[c, :, h],
                pairs_ref[0, :, h],
                (((1,), (1,)), ((), ())),
                preferred_element_type=jnp.float32,
            )
            for h in heads
        ]
        mixed = [(value + value * jnp.tanh(value)).astype(jnp.bfloat16) for value in scores]
        for h, value in zip(heads, mixed):
            attended_ref[r, c, :, h] = jnp.dot(
                value, pairs_ref[1, :, h], preferred_element_type=jnp.float32
            )

    def run_batch(b):
        @pl.loop(0, chunks * chunks)
        def _(t):
            d = t * 0
            for edge in range(1, chunks):
                d = d + (t >= edge * edge).astype(jnp.int32)
            k = t - d * d
            c = jnp.where(k < d, d, k - d)
            r = jnp.where(k < d, k, d)
            i = b * chunks + r

            @pl.when(k == 0)
            def _():
                relay(b * chunks + d)

            @pl.when((k == 0) & (b == 0))
            def _():
                enter_chunk(d)

            @pl.when((k == d) & (b == 0))
            def _():
                at_chunk(MIDDLE, d)

            @pl.when(k == d)
            def _():
                enter_request(i)

            attend(c, r, i)

        @pl.when(b == 0)
        def _():
            hand((last_piece,))
            collect((gate_piece,))
            gate_ref[...] = (
                silu(
                    jnp.dot(
                        items_ref[...].reshape(PARTS * rows, width),
                        gate_weight_ref[...],
                        preferred_element_type=jnp.float32,
                    )
                )
                * gain_ref[...]
            )

        def norm(r):
            length = jnp.full(
                (1, 1), length_ref[part * requests + b * chunks + r], jnp.int32
            ).astype(jnp.float32)
            for p in range(2 * PARTS):
                tile = pl.ds(p * rows // 2, rows // 2)
                attended = jnp.concatenate(
                    [attended_ref[r, c, tile] for c in range(chunks)], axis=-1
                )
                center = attended - jnp.mean(attended, axis=-1, keepdims=True)
                spread = jnp.mean(center * center, axis=-1, keepdims=True)
                normed_ref[r, tile] = (
                    center * lax.rsqrt(spread + EPSILON * length * length) * gate_ref[tile]
                ).astype(jnp.bfloat16)

        norm(0)

        @pl.when(b == 0)
        def _():
            collect((last_piece,))

        for r in range(chunks):
            i = b * chunks + r
            if r + 1 < chunks:
                norm(r + 1)
            merged = (
                jnp.dot(normed_ref[r], last_weight_ref[:, :width], preferred_element_type=jnp.float32)
                + items_ref[...].reshape(PARTS * rows, width).astype(jnp.float32)
            ).astype(jnp.bfloat16)
            hidden = silu(
                jnp.dot(merged, last_weight_ref[:, width:], preferred_element_type=jnp.float32)
            ).astype(jnp.bfloat16)
            logits = lax.dot_general(
                score_weight_ref[...],
                hidden,
                (((1,), (1,)), ((), ())),
                preferred_element_type=jnp.float32,
            )
            for n in range(PARTS * rows // BLOCK):
                logits_ref[lane, part * requests + i, n // (rows // BLOCK), n % (rows // BLOCK)] = (
                    logits[:, n * BLOCK : (n + 1) * BLOCK]
                )

            if r % batch_sends == batch_sends - 1:
                for k, target in enumerate(others):
                    logit_copy(i + 1 - batch_sends, k, target, shard).start()

    if batches == 1:
        run_batch(0)
    else:

        @pl.loop(0, batches)
        def _(b):
            run_batch(b)

    cross_copy().wait_send()
    finish((item_piece, gate_piece, last_piece))

    @pl.loop(0, chunks)
    def _(c):
        finish((chunk_piece(c),))

    @pl.loop(0, requests)
    def _(i):
        for k, target in enumerate(others):

            @pl.when(direct(target))
            def _():
                event_copy(i, k, target, shard).wait_send()

        for k, (middle, _, _) in enumerate(relays):

            @pl.when(shard == middle)
            def _():
                relay_copy(i, k).wait_send()

    @pl.loop(0, requests // batch_sends)
    def _(step):
        for k, target in enumerate(others):
            logit_copy(step * batch_sends, k, target, shard).wait_send()
            logit_copy(step * batch_sends, k, target, target).wait_recv()

    all_requests, max_blocks = block_shard_ref.shape
    per_scorer = max_blocks // shards

    for q in range(all_requests):
        for j in range(per_scorer):
            slot = shard * per_scorer + j
            source = block_shard_ref[q, slot]
            found = logits_ref[
                lax.rem(source, lanes), q, lax.div(source, lanes), block_index_ref[q, slot]
            ]
            for n in range(score_weight_ref.shape[0]):
                picked_ref[n, q : q + 1, j * BLOCK : (j + 1) * BLOCK] = found[n : n + 1]

    row_number = shard * (per_scorer * BLOCK) + lax.broadcasted_iota(jnp.int32, ages_ref.shape, 1)
    decay = decay_ref[...]
    blended = decay * picked_ref[0] + (1.0 - decay) * picked_ref[1]
    scores_ref[...] = jnp.where(row_number < limit_ref[...], blended, 0.0)


def pair_scores(
    length, count, block_shard, block_index, history, items, history_weight, candidate_weight,
    output_weight, hidden_weight, ages, gain, score_weight,
):
    all_requests, own_events, width = history.shape
    rows = items.shape[0]
    groups, shards = lax.axis_size("req"), lax.axis_size("cand")
    history_total = own_events * shards
    requests = all_requests // PARTS
    chunks = HEADS // 2
    span = width // chunks
    depth = history_weight.shape[0] * groups
    pieces = 3 + chunks
    small = pl.BlockSpec(memory_space=pltpu.SMEM)
    whole = pl.BlockSpec(memory_space=pltpu.VMEM)
    apart = pl.BlockSpec(memory_space=pl.ANY)
    sends = requests * LOGIT_SENDS // chunks
    return pl.pallas_call(
        functools.partial(pair_kernel, groups, shards),
        out_shape=jax.ShapeDtypeStruct(ages.shape, jnp.float32),
        in_specs=[small] * 4 + [apart] * 6 + [whole] * 3,
        out_specs=whole,
        scratch_shapes=[
            pltpu.VMEM((requests, history_total, width), jnp.bfloat16),
            pltpu.VMEM((PARTS, rows, width), jnp.bfloat16),
            pltpu.VMEM((chunks, depth, 3 * span), jnp.bfloat16),
            pltpu.VMEM((depth, width), jnp.bfloat16),
            pltpu.VMEM((depth, width + hidden_weight.shape[1]), jnp.bfloat16),
            pltpu.VMEM((chunks, PARTS * rows, span), jnp.bfloat16),
            pltpu.VMEM((PARTS * rows, width), jnp.float32),
            pltpu.VMEM((2, history_total, span), jnp.bfloat16),
            pltpu.VMEM((chunks, chunks, PARTS * rows, span), jnp.float32),
            pltpu.VMEM((chunks, PARTS * rows, width), jnp.bfloat16),
            pltpu.VMEM(
                (
                    shards // PARTS, all_requests, PARTS, rows // BLOCK, score_weight.shape[0],
                    BLOCK,
                ),
                jnp.float32,
            ),
            pltpu.VMEM(ages.shape, jnp.float32),
            pltpu.VMEM(ages.shape, jnp.int32),
            pltpu.VMEM((score_weight.shape[0], *ages.shape), jnp.float32),
            pltpu.SemaphoreType.DMA((pieces, groups // 2)),
            pltpu.SemaphoreType.DMA((pieces, groups)),
            pltpu.SemaphoreType.DMA((pieces, groups // 2)),
            pltpu.SemaphoreType.DMA((pieces, groups // 2)),
            pltpu.SemaphoreType.DMA,
            pltpu.SemaphoreType.DMA,
            pltpu.SemaphoreType.DMA((requests, shards + 1)),
            pltpu.SemaphoreType.DMA((requests, shards)),
            pltpu.SemaphoreType.DMA((sends, shards)),
            pltpu.SemaphoreType.DMA((sends, shards)),
            pltpu.SemaphoreType.DMA((4 + 3 * chunks,)),
            pltpu.SemaphoreType.DMA((requests,)),
        ],
        compiler_params=pltpu.CompilerParams(
            collective_id=0, has_side_effects=True, vmem_limit_bytes=60 * 1024 * 1024
        ),
    )(
        length, count, block_shard, block_index, history, items, history_weight, candidate_weight,
        output_weight, hidden_weight, ages, gain, score_weight,
    )


def local(
    history,
    history_length,
    candidate_count,
    block_shard,
    block_index,
    item_table,
    item_ages,
    history_weight,
    candidate_weight,
    output_weight,
    hidden_weight,
    norm_gain,
    score_weight,
):
    return pair_scores(
        history_length,
        candidate_count,
        block_shard,
        block_index,
        history,
        item_table.reshape(-1, item_table.shape[2]),
        history_weight,
        candidate_weight,
        output_weight,
        hidden_weight,
        item_ages,
        norm_gain[None, :],
        score_weight,
    )


def solution(mesh):
    return jax.shard_map(
        local,
        mesh=mesh,
        in_specs=(
            P("req", "cand", None),
            P("req"),
            P("req"),
            P("req", None),
            P("req", None),
            P("cand", None, None),
            P("req", "cand"),
            P("req", None),
            P("req", None),
            P("req", None),
            P("req", None),
            P(),
            P(),
        ),
        out_specs=P("req", "cand"),
        check_vma=False,
    )
```

```python
import functools
import math

import jax
import jax.numpy as jnp
from jax import lax
from jax.experimental import pallas as pl
from jax.experimental.pallas import tpu as pltpu
from jax.sharding import PartitionSpec as P

HEADS = 8
BLOCK = 128
EPSILON = 1e-05
AGE_SCALE = 48.0
PARTS = 2
LOGIT_SENDS = 2
ENTER = {1: [('send', 4)], 2: [('send', 5)]}
MIDDLE = {0: [('hand', 1), ('turn', 2)], 1: [('hand', 2), ('turn', 3)], 2: [('hand', 3), ('turn', 4)], 3: [('hand', 4), ('turn', 5)]}


def silu(value):
    half = 0.5 * value
    return half + half * jnp.tanh(half)


MESH = pl.DeviceIdType.MESH


def pair_kernel(
    groups,
    shards,
    length_ref,
    count_ref,
    block_shard_ref,
    block_index_ref,
    history_ref,
    item_shard_ref,
    history_shard_ref,
    candidate_shard_ref,
    output_shard_ref,
    hidden_shard_ref,
    ages_ref,
    gain_ref,
    score_weight_ref,
    scores_ref,
    events_ref,
    items_ref,
    chunk_weight_ref,
    gate_weight_ref,
    last_weight_ref,
    query_ref,
    gate_ref,
    pairs_ref,
    attended_ref,
    normed_ref,
    logits_ref,
    decay_ref,
    limit_ref,
    picked_ref,
    weight_send,
    weight_recv,
    pass_send,
    turn_send,
    cross_send,
    cross_recv,
    event_send,
    event_recv,
    logit_send,
    logit_recv,
    own_sem,
    own_event_sem,
):
    group = lax.axis_index("req")
    shard = lax.axis_index("cand")
    partner = group + 1 - 2 * lax.rem(group, 2)
    own_events = history_ref.shape[1]
    width = history_ref.shape[2]
    lanes = shards // PARTS
    part, lane = lax.div(shard, lanes), lax.rem(shard, lanes)
    mate = lax.rem(shard + lanes, shards)
    requests, history_total = events_ref.shape[:2]
    chunks, _, span = query_ref.shape
    batch_sends = chunks // LOGIT_SENDS
    batches = requests // chunks
    rows = item_shard_ref.shape[0]
    head = width // HEADS
    half_scale = 0.5 / math.sqrt(head)
    depth = history_shard_ref.shape[0]
    item_depth = rows // groups
    half = groups // 2
    row, core = lax.div(group, half), lax.rem(group, 2)
    across = lax.rem(group + half, groups)
    beside = [row * half + lax.rem(group - row * half + 2 * d, half) for d in range(1, half // 2)]
    diagonal = [lax.rem(source + half, groups) for source in beside]
    near = (*beside, across)
    same_core = (*near, *diagonal)
    partner_core = [source + partner - group for source in same_core]
    others = [lax.rem(shard + d, shards) for d in range(1, shards)]
    relays = ((1, 2, 0), (2, 1, 3)) if shards == 4 else ()

    def rows_of(source):
        return pl.ds(pl.multiple_of(source * depth, depth), depth)

    def item_rows(source):
        return pl.ds(pl.multiple_of(source * item_depth, item_depth), item_depth)

    def events_of(source):
        return pl.ds(pl.multiple_of(source * own_events, own_events), own_events)

    def columns(start):
        return pl.ds(pl.multiple_of(start, span), span)

    item_piece = (0, lambda source: items_ref.at[1 - part, item_rows(source)])
    gate_piece = (1, lambda source: gate_weight_ref.at[rows_of(source)])
    last_piece = (2, lambda source: last_weight_ref.at[rows_of(source)])

    def chunk_piece(c):
        return (3 + c, lambda source: chunk_weight_ref.at[c, rows_of(source)])

    def weight_copy(piece, k, target, source):
        w, place = piece
        return pltpu.make_async_remote_copy(
            src_ref=place(source),
            dst_ref=place(source),
            send_sem=weight_send.at[w, k],
            recv_sem=weight_recv.at[w, source],
            device_id={"req": target},
            device_id_type=MESH,
        )

    def pass_copy(piece, k, source):
        w, place = piece
        return pltpu.make_async_remote_copy(
            src_ref=place(source),
            dst_ref=place(source),
            send_sem=pass_send.at[w, k],
            recv_sem=weight_recv.at[w, source],
            device_id={"req": partner},
            device_id_type=MESH,
        )

    def turn_copy(piece, k):
        w, place = piece
        source = beside[k] + core * (across - beside[k])
        target = across + core * (beside[k] - across)
        return pltpu.make_async_remote_copy(
            src_ref=place(source),
            dst_ref=place(source),
            send_sem=turn_send.at[w, k],
            recv_sem=weight_recv.at[w, source],
            device_id={"req": target},
            device_id_type=MESH,
        )

    def own_parts():
        own = rows_of(group)
        parts = [(item_shard_ref, items_ref.at[part])]
        for c in range(chunks):
            for k, (shard_ref, start) in enumerate(
                ((candidate_shard_ref, 0), (history_shard_ref, 0), (history_shard_ref, width))
            ):
                parts.append(
                    (
                        shard_ref.at[:, pl.ds(start + c * span, span)],
                        chunk_weight_ref.at[c, own, pl.ds(k * span, span)],
                    )
                )
        parts.append((candidate_shard_ref.at[:, pl.ds(width, width)], gate_weight_ref.at[own]))
        parts.append((output_shard_ref, last_weight_ref.at[own, pl.ds(0, width)]))
        parts.append(
            (hidden_shard_ref, last_weight_ref.at[own, pl.ds(width, hidden_shard_ref.shape[1])])
        )
        return [
            pltpu.make_async_copy(source, target, own_sem.at[k])
            for k, (source, target) in enumerate(parts)
        ]

    def send(pieces):
        for piece in pieces:
            for k, target in enumerate((*near, partner)):
                weight_copy(piece, k, target, group).start()

    def arrive(piece, sources):
        for source in sources:
            weight_copy(piece, 0, partner, source).wait_recv()

    def turn(pieces):
        for piece in pieces:
            arrive(piece, near)
            for k in range(len(beside)):
                turn_copy(piece, k).start()
            for k, source in enumerate(near):
                pass_copy(piece, k, source).start()

    def hand(pieces):
        for piece in pieces:
            arrive(piece, diagonal)
            for k, source in enumerate(diagonal):
                pass_copy(piece, len(near) + k, source).start()

    def collect(pieces):
        for piece in pieces:
            arrive(piece, (partner, *partner_core))

    def finish(pieces):
        for piece in pieces:
            for k, target in enumerate((*near, partner)):
                weight_copy(piece, k, target, group).wait_send()
            for k, source in enumerate(same_core):
                pass_copy(piece, k, source).wait_send()
            for k in range(len(beside)):
                turn_copy(piece, k).wait_send()

    def cross_copy():
        return pltpu.make_async_remote_copy(
            src_ref=item_shard_ref.at[item_rows(group)],
            dst_ref=items_ref.at[part, item_rows(group)],
            send_sem=cross_send,
            recv_sem=cross_recv,
            device_id={"cand": mate},
            device_id_type=MESH,
        )

    def cross_arrival():
        return pltpu.make_async_remote_copy(
            src_ref=item_shard_ref.at[item_rows(group)],
            dst_ref=items_ref.at[1 - part, item_rows(group)],
            send_sem=cross_send,
            recv_sem=cross_recv,
            device_id={"cand": mate},
            device_id_type=MESH,
        )

    def event_copy(i, k, target, source):
        return pltpu.make_async_remote_copy(
            src_ref=history_ref.at[lax.div(target, lanes) * requests + i],
            dst_ref=events_ref.at[i, events_of(source)],
            send_sem=event_send.at[i, k],
            recv_sem=event_recv.at[i, source],
            device_id={"cand": target},
            device_id_type=MESH,
        )

    def relay_copy(i, k):
        _, source, target = relays[k]
        return pltpu.make_async_remote_copy(
            src_ref=events_ref.at[i, events_of(source)],
            dst_ref=events_ref.at[i, events_of(source)],
            send_sem=event_send.at[i, len(others) + k],
            recv_sem=event_recv.at[i, source],
            device_id={"cand": target},
            device_id_type=MESH,
        )

    def direct(target):
        flag = shard >= 0
        for _, source, end in relays:
            flag = flag & ((shard != source) | (target != end))
        return flag

    def own_event(i):
        return pltpu.make_async_copy(
            history_ref.at[part * requests + i],
            events_ref.at[i, events_of(shard)],
            own_event_sem.at[i],
        )

    def logit_copy(first, k, target, source):
        place = logits_ref.at[
            lax.rem(source, lanes), pl.ds(lax.div(source, lanes) * requests + first, batch_sends)
        ]
        step = lax.div(first, batch_sends)
        return pltpu.make_async_remote_copy(
            src_ref=place,
            dst_ref=place,
            send_sem=logit_send.at[step, k],
            recv_sem=logit_recv.at[step, source],
            device_id={"cand": target},
            device_id_type=MESH,
        )

    own = own_parts()
    for copy in own:
        copy.start()

    barrier = pltpu.get_barrier_semaphore()
    for target in (*near, partner):
        pl.semaphore_signal(barrier, inc=1, device_id={"req": target}, device_id_type=MESH)
    for target in others:
        pl.semaphore_signal(barrier, inc=1, device_id={"cand": target}, device_id_type=MESH)
    pl.semaphore_wait(barrier, len(near) + 1 + len(others))

    late = {-1: item_piece, chunks: gate_piece, chunks + 1: last_piece}

    def piece_at(level):
        return late[level] if level in late else chunk_piece(level)

    def run_steps(steps):
        for action, level in steps:
            {"send": send, "turn": turn, "hand": hand}[action]((piece_at(level),))

    def at_chunk(table, d):
        for edge, steps in table.items():

            @pl.when(d == edge)
            def _():
                run_steps(steps)

    def send_events(i):
        for k, target in enumerate(others):

            @pl.when(direct(target))
            def _():
                event_copy(i, k, target, shard).start()

        own_event(i).start()

    for copy in own:
        copy.wait()
    send((chunk_piece(0),))
    cross_copy().start()
    send((chunk_piece(1),))

    @pl.loop(0, requests)
    def _(i):
        send_events(i)

    decay_ref[...] = jnp.exp(-ages_ref[...].astype(jnp.float32) / AGE_SCALE)
    for q in range(count_ref.shape[0]):
        limit_ref[q : q + 1] = jnp.full((1, limit_ref.shape[1]), count_ref[q], jnp.int32)
    turn((chunk_piece(0),))
    cross_arrival().wait_recv()
    send((item_piece,))
    send((chunk_piece(2),))
    turn((chunk_piece(1),))
    hand((chunk_piece(0),))
    turn((item_piece,))
    hand((item_piece,))
    send((chunk_piece(3),))
    collect((item_piece,))

    def enter_chunk(d):
        at_chunk(ENTER, d)
        collect((chunk_piece(d),))
        query_ref[d] = (
            half_scale
            * silu(
                jnp.dot(
                    items_ref[...].reshape(PARTS * rows, width),
                    chunk_weight_ref[d, :, :span],
                    preferred_element_type=jnp.float32,
                )
            )
        ).astype(jnp.bfloat16)

    def relay(i):
        for k, (middle, source, _) in enumerate(relays):

            @pl.when(shard == middle)
            def _():
                event_copy(i, 0, mate, source).wait_recv()
                relay_copy(i, k).start()

    def relayed(source):
        flag = shard < 0
        for middle, start, _ in relays:
            flag = flag | ((shard == middle) & (source == start))
        return flag

    def enter_request(i):
        own_event(i).wait()
        for source in others:

            @pl.when(jnp.logical_not(relayed(source)))
            def _():
                event_copy(i, 0, mate, source).wait_recv()

    def attend(c, r, i):
        length = length_ref[part * requests + i]
        events = events_ref[i]
        pairs_ref[0] = silu(
            jnp.dot(
                events,
                chunk_weight_ref[c, :, span : 2 * span],
                preferred_element_type=jnp.float32,
            )
        ).astype(jnp.bfloat16)
        live = lax.broadcasted_iota(jnp.int32, (history_total, span), 0) < length
        pairs_ref[1] = jnp.where(
            live,
            silu(
                jnp.dot(
                    events,
                    chunk_weight_ref[c, :, 2 * span :],
                    preferred_element_type=jnp.float32,
                )
            ),
            0.0,
        ).astype(jnp.bfloat16)
        heads = [slice(h * head, (h + 1) * head) for h in range(span // head)]
        scores = [
            lax.dot_general(
                query_ref[c, :, h],
                pairs_ref[0, :, h],
                (((1,), (1,)), ((), ())),
                preferred_element_type=jnp.float32,
            )
            for h in heads
        ]
        mixed = [(value + value * jnp.tanh(value)).astype(jnp.bfloat16) for value in scores]
        for h, value in zip(heads, mixed):
            attended_ref[r, c, :, h] = jnp.dot(
                value, pairs_ref[1, :, h], preferred_element_type=jnp.float32
            )

    def run_batch(b):
        @pl.loop(0, chunks * chunks)
        def _(t):
            d = t * 0
            for edge in range(1, chunks):
                d = d + (t >= edge * edge).astype(jnp.int32)
            k = t - d * d
            c = jnp.where(k < d, d, k - d)
            r = jnp.where(k < d, k, d)
            i = b * chunks + r

            @pl.when(k == 0)
            def _():
                relay(b * chunks + d)

            @pl.when((k == 0) & (b == 0))
            def _():
                enter_chunk(d)

            @pl.when((k == d) & (b == 0))
            def _():
                at_chunk(MIDDLE, d)

            @pl.when(k == d)
            def _():
                enter_request(i)

            @pl.when((t + 2 == chunks * chunks) & (b == 0))
            def _():
                collect((gate_piece,))
                gate_ref[...] = (
                    silu(
                        jnp.dot(
                            items_ref[...].reshape(PARTS * rows, width),
                            gate_weight_ref[...],
                            preferred_element_type=jnp.float32,
                        )
                    )
                    * gain_ref[...]
                )

            attend(c, r, i)

        @pl.when(b == 0)
        def _():
            hand((last_piece,))

        def norm(r):
            length = jnp.full(
                (1, 1), length_ref[part * requests + b * chunks + r], jnp.int32
            ).astype(jnp.float32)
            for p in range(2 * PARTS):
                tile = pl.ds(p * rows // 2, rows // 2)
                attended = jnp.concatenate(
                    [attended_ref[r, c, tile] for c in range(chunks)], axis=-1
                )
                center = attended - jnp.mean(attended, axis=-1, keepdims=True)
                spread = jnp.mean(center * center, axis=-1, keepdims=True)
                normed_ref[r, tile] = (
                    center * lax.rsqrt(spread + EPSILON * length * length) * gate_ref[tile]
                ).astype(jnp.bfloat16)

        norm(0)

        @pl.when(b == 0)
        def _():
            collect((last_piece,))

        for r in range(chunks):
            i = b * chunks + r
            if r + 1 < chunks:
                norm(r + 1)
            merged = (
                jnp.dot(normed_ref[r], last_weight_ref[:, :width], preferred_element_type=jnp.float32)
                + items_ref[...].reshape(PARTS * rows, width).astype(jnp.float32)
            ).astype(jnp.bfloat16)
            hidden = silu(
                jnp.dot(merged, last_weight_ref[:, width:], preferred_element_type=jnp.float32)
            ).astype(jnp.bfloat16)
            logits = lax.dot_general(
                score_weight_ref[...],
                hidden,
                (((1,), (1,)), ((), ())),
                preferred_element_type=jnp.float32,
            )
            for n in range(PARTS * rows // BLOCK):
                logits_ref[lane, part * requests + i, n // (rows // BLOCK), n % (rows // BLOCK)] = (
                    logits[:, n * BLOCK : (n + 1) * BLOCK]
                )

            if r % batch_sends == batch_sends - 1:
                for k, target in enumerate(others):
                    logit_copy(i + 1 - batch_sends, k, target, shard).start()

    if batches == 1:
        run_batch(0)
    else:

        @pl.loop(0, batches)
        def _(b):
            run_batch(b)

    cross_copy().wait_send()
    finish((item_piece, gate_piece, last_piece))

    @pl.loop(0, chunks)
    def _(c):
        finish((chunk_piece(c),))

    @pl.loop(0, requests)
    def _(i):
        for k, target in enumerate(others):

            @pl.when(direct(target))
            def _():
                event_copy(i, k, target, shard).wait_send()

        for k, (middle, _, _) in enumerate(relays):

            @pl.when(shard == middle)
            def _():
                relay_copy(i, k).wait_send()

    @pl.loop(0, requests // batch_sends)
    def _(step):
        for k, target in enumerate(others):
            logit_copy(step * batch_sends, k, target, shard).wait_send()
            logit_copy(step * batch_sends, k, target, target).wait_recv()

    all_requests, max_blocks = block_shard_ref.shape
    per_scorer = max_blocks // shards

    for q in range(all_requests):
        for j in range(per_scorer):
            slot = shard * per_scorer + j
            source = block_shard_ref[q, slot]
            found = logits_ref[
                lax.rem(source, lanes), q, lax.div(source, lanes), block_index_ref[q, slot]
            ]
            for n in range(score_weight_ref.shape[0]):
                picked_ref[n, q : q + 1, j * BLOCK : (j + 1) * BLOCK] = found[n : n + 1]

    row_number = shard * (per_scorer * BLOCK) + lax.broadcasted_iota(jnp.int32, ages_ref.shape, 1)
    decay = decay_ref[...]
    blended = decay * picked_ref[0] + (1.0 - decay) * picked_ref[1]
    scores_ref[...] = jnp.where(row_number < limit_ref[...], blended, 0.0)


def pair_scores(
    length, count, block_shard, block_index, history, items, history_weight, candidate_weight,
    output_weight, hidden_weight, ages, gain, score_weight,
):
    all_requests, own_events, width = history.shape
    rows = items.shape[0]
    groups, shards = lax.axis_size("req"), lax.axis_size("cand")
    history_total = own_events * shards
    requests = all_requests // PARTS
    chunks = HEADS // 2
    span = width // chunks
    depth = history_weight.shape[0] * groups
    pieces = 3 + chunks
    small = pl.BlockSpec(memory_space=pltpu.SMEM)
    whole = pl.BlockSpec(memory_space=pltpu.VMEM)
    apart = pl.BlockSpec(memory_space=pl.ANY)
    sends = requests * LOGIT_SENDS // chunks
    return pl.pallas_call(
        functools.partial(pair_kernel, groups, shards),
        out_shape=jax.ShapeDtypeStruct(ages.shape, jnp.float32),
        in_specs=[small] * 4 + [apart] * 6 + [whole] * 3,
        out_specs=whole,
        scratch_shapes=[
            pltpu.VMEM((requests, history_total, width), jnp.bfloat16),
            pltpu.VMEM((PARTS, rows, width), jnp.bfloat16),
            pltpu.VMEM((chunks, depth, 3 * span), jnp.bfloat16),
            pltpu.VMEM((depth, width), jnp.bfloat16),
            pltpu.VMEM((depth, width + hidden_weight.shape[1]), jnp.bfloat16),
            pltpu.VMEM((chunks, PARTS * rows, span), jnp.bfloat16),
            pltpu.VMEM((PARTS * rows, width), jnp.float32),
            pltpu.VMEM((2, history_total, span), jnp.bfloat16),
            pltpu.VMEM((chunks, chunks, PARTS * rows, span), jnp.float32),
            pltpu.VMEM((chunks, PARTS * rows, width), jnp.bfloat16),
            pltpu.VMEM(
                (
                    shards // PARTS, all_requests, PARTS, rows // BLOCK, score_weight.shape[0],
                    BLOCK,
                ),
                jnp.float32,
            ),
            pltpu.VMEM(ages.shape, jnp.float32),
            pltpu.VMEM(ages.shape, jnp.int32),
            pltpu.VMEM((score_weight.shape[0], *ages.shape), jnp.float32),
            pltpu.SemaphoreType.DMA((pieces, groups // 2)),
            pltpu.SemaphoreType.DMA((pieces, groups)),
            pltpu.SemaphoreType.DMA((pieces, groups // 2)),
            pltpu.SemaphoreType.DMA((pieces, groups // 2)),
            pltpu.SemaphoreType.DMA,
            pltpu.SemaphoreType.DMA,
            pltpu.SemaphoreType.DMA((requests, shards + 1)),
            pltpu.SemaphoreType.DMA((requests, shards)),
            pltpu.SemaphoreType.DMA((sends, shards)),
            pltpu.SemaphoreType.DMA((sends, shards)),
            pltpu.SemaphoreType.DMA((4 + 3 * chunks,)),
            pltpu.SemaphoreType.DMA((requests,)),
        ],
        compiler_params=pltpu.CompilerParams(
            collective_id=0, has_side_effects=True, vmem_limit_bytes=60 * 1024 * 1024
        ),
    )(
        length, count, block_shard, block_index, history, items, history_weight, candidate_weight,
        output_weight, hidden_weight, ages, gain, score_weight,
    )


def local(
    history,
    history_length,
    candidate_count,
    block_shard,
    block_index,
    item_table,
    item_ages,
    history_weight,
    candidate_weight,
    output_weight,
    hidden_weight,
    norm_gain,
    score_weight,
):
    return pair_scores(
        history_length,
        candidate_count,
        block_shard,
        block_index,
        history,
        item_table.reshape(-1, item_table.shape[2]),
        history_weight,
        candidate_weight,
        output_weight,
        hidden_weight,
        item_ages,
        norm_gain[None, :],
        score_weight,
    )


def solution(mesh):
    return jax.shard_map(
        local,
        mesh=mesh,
        in_specs=(
            P("req", "cand", None),
            P("req"),
            P("req"),
            P("req", None),
            P("req", None),
            P("cand", None, None),
            P("req", "cand"),
            P("req", None),
            P("req", None),
            P("req", None),
            P("req", None),
            P(),
            P(),
        ),
        out_specs=P("req", "cand"),
        check_vma=False,
    )
```
